256 devices in a mesh: dp: 2 (over x_hi), head: 8 (over z), frame: 16 (over y, x_lo, core).
Axes of the slice: x: 4 (x_hi: 2, x_lo: 2; x = x_hi * 2 + x_lo), y: 4, z: 8, core: 2. Of those that a mesh axis runs over, the one named last changes fastest.
Arguments:
- queries: bfloat16 [8192, 5120], P(('dp', 'frame', 'head')), parts along dimension 0, may hold values from -5 to 5
- keys: bfloat16 [8192, 5120], P(('dp', 'frame', 'head')), parts along dimension 0, may hold values from -5 to 5
- values: bfloat16 [8192, 5120], P(('dp', 'frame', 'head')), parts along dimension 0, may hold values from -6 to 6
- out_grad: bfloat16 [8192, 5120], P(('dp', 'frame', 'head')), parts along dimension 0, may hold values from -6 to 6
- tile_mask: int32 [40, 32, 32], P('head'), may hold values from 0 to 1, as said below
Outputs:
- attended: bfloat16 [8192, 5120], P(('dp', 'frame'), 'head'), parts along dimension 0
- query_grad: bfloat16 [8192, 5120], P(('dp', 'frame'), 'head'), parts along dimension 0
- key_grad: bfloat16 [8192, 5120], P(('dp', 'frame'), 'head'), parts along dimension 0
- value_grad: bfloat16 [8192, 5120], P(('dp', 'frame'), 'head'), parts along dimension 0
The draws below stay inside these ranges and needn't reach their ends.
There are 2 independent parts, one for each index of `dp`. The reference program is written for one: setup_inputs(seed, part) draws one part's arguments, and reference() takes and returns one part's arrays. A program takes and returns all parts, laid end to end along the dimension named above; an argument that names none is the same for every part. Nothing has to cross between parts.
Inputs may be any that keep to these rules, and one draw needn't show every extreme that they name: tile_mask[h, i, i] = 1 for every head h and tile i.
All inputs are finite; a program needn't handle non-finite values.
Results may differ from the reference program's by a relative error of at most 0.022.
Values may be sent and summed in bfloat16 or wider, within the bound.
A program may use at most 128 MiB of HBM per device.

```python
import math
import jax
import jax.numpy as jnp
from jax import lax

H = 40
HD = 128
D = 5120
TILE = 128
SLAB = 256
TOKENS = 4096
NB = 32


def paired_fields(key):
    base = jax.random.fold_in(key, 7)
    first, second = jax.random.split(base, 2)
    query_field = jax.random.truncated_normal(first, -4.5, 4.5, (TOKENS, D), jnp.float32)
    key_field = jax.random.truncated_normal(second, -4.5, 4.5, (TOKENS, D), jnp.float32)
    return (query_field, key_field)


def draw_queries(key, part):
    return paired_fields(key)[0].astype(jnp.bfloat16)


def draw_keys(key, part):
    return paired_fields(key)[1].astype(jnp.bfloat16)


def draw_tile_mask(key, part):
    base = jax.random.fold_in(key, 11)
    first, second = jax.random.split(base, 2)
    level = jax.random.randint(first, (H, 1, 1), 0, 6)
    threshold = jnp.left_shift(jnp.int32(1), level)
    rolls = jax.random.randint(second, (H, NB, NB), 0, 64)
    diagonal = jnp.arange(NB)[:, None] == jnp.arange(NB)[None, :]
    return jnp.where(diagonal[None, :, :] | (rolls < threshold), 1, 0).astype(jnp.int32)


def level_of(stream_key, extent, cuts, low, high):
    factor_of, own = 1.0, jax.random.fold_in(stream_key, 6)
    for dim, parts in cuts:
        draws = jnp.exp(jax.random.uniform(jax.random.fold_in(own, dim), (parts,), jnp.float32, low / len(cuts), high / len(cuts)))
        factor_of = factor_of * jnp.repeat(draws, extent[dim] // parts).reshape([-1 if axis == dim else 1 for axis in range(len(extent))])
    return factor_of


def scatter_about(stream_key, dims, spread, most, cuts=(), kind=jnp.bfloat16):
    level = level_of(stream_key, dims, cuts, -0.22, 0.18) if cuts else 1.0
    drawn = jax.random.normal(stream_key, dims, jnp.float32) * spread * level
    return jnp.minimum(jnp.maximum(drawn, -most), most).astype(kind)


def setup_inputs(seed: int = 0, part: int = 0) -> dict:
    key_list = jax.random.split(jax.random.key(seed), 6)
    own_keys = jax.random.split(jax.random.fold_in(key_list[5], part), 6)
    return {
        "queries": draw_queries(jax.random.fold_in(jax.random.fold_in(key_list[5], part), 71), part),
        "keys": draw_keys(jax.random.fold_in(jax.random.fold_in(key_list[5], part), 71), part),
        "values": scatter_about(own_keys[2], (TOKENS, D), 1.0, 6.0, ((0, 128),)),
        "out_grad": scatter_about(own_keys[3], (TOKENS, D), 1.0, 6.0, ((0, 128),)),
        "tile_mask": draw_tile_mask(jax.random.fold_in(key_list[5], 71), part),
    }


EXCLUDED = -1e+30

def head_pass(inputs):
    query_head, key_head, value_head, grad_head, mask_head = inputs
    scaling = 1.0 / math.sqrt(HD)
    scores = jnp.dot(query_head, key_head.T, preferred_element_type=jnp.float32) * scaling
    allowed = jnp.repeat(jnp.repeat(mask_head, TILE, axis=0), TILE, axis=1) == 1
    masked = jnp.where(allowed, scores, EXCLUDED)
    peak = lax.optimization_barrier(jnp.max(masked, axis=1))
    weights = jnp.where(allowed, jnp.exp(masked - peak[:, None]), 0.0)
    totals = lax.optimization_barrier(jnp.sum(weights, axis=1))
    attended = (jnp.dot(weights.astype(jnp.bfloat16), value_head, preferred_element_type=jnp.float32) / totals[:, None]).astype(jnp.bfloat16)
    logsum = peak + jnp.log(totals)
    out_delta = lax.optimization_barrier(jnp.sum(grad_head.astype(jnp.float32) * attended.astype(jnp.float32), axis=1))
    probabilities = jnp.where(allowed, jnp.exp(masked - logsum[:, None]), 0.0)
    prob_grad = jnp.dot(grad_head, value_head.T, preferred_element_type=jnp.float32)
    score_grad = probabilities * (prob_grad - out_delta[:, None])
    probs_half = lax.optimization_barrier(probabilities.astype(jnp.bfloat16))
    score_half = lax.optimization_barrier(score_grad.astype(jnp.bfloat16))
    query_grad = (jnp.dot(score_half, key_head, preferred_element_type=jnp.float32) * scaling).astype(jnp.bfloat16)
    slab_count = TOKENS // SLAB
    grad_slabs = grad_head.astype(jnp.float32).reshape(slab_count, SLAB, HD)
    query_slabs = query_head.astype(jnp.float32).reshape(slab_count, SLAB, HD)
    value_parts = jnp.einsum('sqk,sqd->skd', probs_half.astype(jnp.float32).reshape(slab_count, SLAB, TOKENS), grad_slabs)
    value_parts = lax.optimization_barrier(value_parts.astype(jnp.bfloat16))
    value_grad = lax.optimization_barrier(jnp.sum(value_parts.astype(jnp.float32), axis=0)).astype(jnp.bfloat16)
    key_parts = jnp.einsum('sqk,sqd->skd', score_half.astype(jnp.float32).reshape(slab_count, SLAB, TOKENS), query_slabs) * scaling
    key_parts = lax.optimization_barrier(key_parts.astype(jnp.bfloat16))
    key_grad = lax.optimization_barrier(jnp.sum(key_parts.astype(jnp.float32), axis=0)).astype(jnp.bfloat16)
    return (attended, query_grad, key_grad, value_grad)

def split_heads(field):
    return field.reshape(TOKENS, H, HD).transpose(1, 0, 2)

def join_heads(field):
    return field.transpose(1, 0, 2).reshape(TOKENS, H * HD)

def reference(queries, keys, values, out_grad, tile_mask):
    results = lax.map(head_pass, (split_heads(queries), split_heads(keys), split_heads(values), split_heads(out_grad), tile_mask))
    return (join_heads(results[0]), join_heads(results[1]), join_heads(results[2]), join_heads(results[3]))
```

```python
import functools
import math

import jax
import jax.numpy as jnp
from jax import lax
from jax.experimental import pallas as pl
from jax.experimental.pallas import tpu as pltpu
from jax.sharding import PartitionSpec as P

HD = 128
TILE = 128
NEG = -1e30
FLOOR = -1e20
LOG2E = 1.4426950408889634
MESH = pl.DeviceIdType.MESH
F32 = jnp.float32
BF16 = jnp.bfloat16

NT = (((1,), (1,)), ((), ()))
NN = (((1,), (0,)), ((), ()))
TN = (((0,), (0,)), ((), ()))

Q, K, V, G = 0, 1, 2, 3


def dot(a, b, dims):
    return lax.dot_general(a, b, dims, preferred_element_type=F32)


def kernel(
    groups,
    q_hbm, k_hbm, v_hbm, g_hbm, mask_ref,
    att_out, dq_out, dk_out, dv_out,
    allx, probs, grads, bias, rows, stats, facts, afacts,
    att_send, dq_send, dk_send, dv_send, out_recv, scaled,
    a2a_send, a2a_recv, own_sem, fwd_send, fwd_recv, st_send, st_recv, out_send, out_rsem,
):
    z = lax.axis_index("head")
    nz = lax.axis_size("head")
    f = lax.axis_index("frame")
    y, xc = f // 4, f % 4
    chunk = q_hbm.shape[0]
    slab = chunk * nz
    width = groups * HD
    scaling = 1.0 / math.sqrt(HD)
    c2 = scaling * LOG2E
    inputs = (q_hbm, k_hbm, v_hbm, g_hbm)

    def head_peer(d):
        return lax.rem(z + d, nz)

    def y_peer(i):
        return lax.rem(y + i, 4) * 4 + xc

    def q_peer(i):
        return y * 4 + lax.rem(xc + i, 4)

    barrier = pltpu.get_barrier_semaphore()
    for d in range(1, nz):
        pl.semaphore_signal(barrier, inc=1, device_id={"head": head_peer(d)}, device_id_type=MESH)
    for i in range(1, 4):
        pl.semaphore_signal(barrier, inc=1, device_id={"frame": y_peer(i)}, device_id_type=MESH)
        pl.semaphore_signal(barrier, inc=1, device_id={"frame": q_peer(i)}, device_id_type=MESH)
    pl.semaphore_wait(barrier, nz - 1 + 6)

    def own_slot(a):
        return y if a in (Q, G) else xc

    def peer(a, i):
        return y_peer(i) if a in (Q, G) else q_peer(i)

    def source_slot(a, i):
        return lax.rem((y if a in (Q, G) else xc) + 4 - i, 4)

    def a2a(a, d):
        to = head_peer(d)
        return pltpu.make_async_remote_copy(
            src_ref=inputs[a].at[:, pl.ds(pl.multiple_of(to * width, width), width)],
            dst_ref=allx.at[a, own_slot(a), pl.ds(pl.multiple_of(z * chunk, chunk), chunk), :],
            send_sem=a2a_send.at[a, d],
            recv_sem=a2a_recv.at[a, d],
            device_id={"head": to},
            device_id_type=MESH,
        )

    def own(a):
        return pltpu.make_async_copy(
            inputs[a].at[:, pl.ds(pl.multiple_of(z * width, width), width)],
            allx.at[a, own_slot(a), pl.ds(pl.multiple_of(z * chunk, chunk), chunk), :],
            own_sem.at[a],
        )

    order = [0]
    for d in range(1, nz // 2 + 1):
        order += [d] if d == nz - d else [d, nz - d]

    for pair in ((K, Q), (V, G)):
        for a in pair:
            own(a).start()
        for d in order[1:]:
            for a in pair:
                a2a(a, d).start()

    def forward(a, d):
        source = lax.rem(z + nz - d, nz)
        part = pl.ds(pl.multiple_of(source * chunk, chunk), chunk)
        for i in (1, 2, 3):
            here = allx.at[a, own_slot(a), part, :]
            pltpu.make_async_remote_copy(
                src_ref=here,
                dst_ref=here,
                send_sem=fwd_send.at[a, i - 1],
                recv_sem=fwd_recv.at[a, i - 1],
                device_id={"frame": peer(a, i)},
                device_id_type=MESH,
            ).start()

    def pass_on(a, d):
        if d == 0:
            own(a).wait()
        else:
            a2a(a, d).wait_recv()
        forward(a, d)

    def slab_copy(a, i):
        return pltpu.make_async_remote_copy(
            src_ref=allx.at[a, own_slot(a)],
            dst_ref=allx.at[a, source_slot(a, i)],
            send_sem=fwd_send.at[a, i - 1],
            recv_sem=fwd_recv.at[a, i - 1],
            device_id={"frame": peer(a, i)},
            device_id_type=MESH,
        )

    def bias_row(row, carry):
        h, qt = row // 8, lax.rem(row, 8)
        qi = (qt // 2) * 8 + xc * 2 + lax.rem(qt, 2)
        for kt in range(8):
            live = mask_ref[h, qi, y * 8 + kt]
            value = jnp.where(live == 1, 0.0, NEG).astype(F32)
            bias[row, :, kt * TILE:(kt + 1) * TILE] = jnp.full((8, TILE), value, F32)
        return carry

    lax.fori_loop(0, groups * 8, bias_row, 0)

    for d in order:
        for a in (K, Q):
            pass_on(a, d)
    for a in (K, Q):
        for i in (1, 2, 3):
            slab_copy(a, i).wait_recv()

    lane = lax.broadcasted_iota(jnp.int32, (slab, HD), 1)

    def softmax_step(unit):
        h, s = unit // 4, lax.rem(unit, 4)
        cols = pl.ds(pl.multiple_of(h * HD, HD), HD)
        query = allx[Q, s, :, cols]
        key = allx[K, :, :, cols].reshape(4 * slab, HD)
        raw = dot(query, key, NT) * c2
        top = raw[:TILE] + bias[h * 8 + 2 * s, 0:1, :]
        low = raw[TILE:] + bias[h * 8 + 2 * s + 1, 0:1, :]
        for part, block in ((0, top), (1, low)):
            peak = jnp.maximum(jnp.max(block, axis=1, keepdims=True), FLOOR)
            weight = jnp.exp2(block - peak)
            total = jnp.sum(weight, axis=1, keepdims=True)
            probs[unit, part * TILE:(part + 1) * TILE, :] = weight.astype(BF16)
            here = pl.ds(part * TILE, TILE)
            old = rows[s, here, :]
            ln = lane[:TILE]
            rows[s, here, :] = jnp.where(ln == h, peak, jnp.where(ln == 8 + h, total, old))

    rows[...] = jnp.zeros_like(rows)
    for step in range(nz):
        for a in (V, G):
            pass_on(a, order[step])

        def two(j, carry, step=step):
            softmax_step(step * 2 + j)
            return carry

        lax.fori_loop(0, 2, two, 0)

    def rest(j, carry):
        softmax_step(j)
        return carry

    lax.fori_loop(2 * nz, groups * 4, rest, 0)

    for a in (V, G):
        for i in (1, 2, 3):
            slab_copy(a, i).wait_recv()

    def out_copy(kind, i, h):
        buffer = (att_send, dq_send, dk_send, dv_send)[kind]
        along = y if kind < 2 else xc
        return pltpu.make_async_remote_copy(
            src_ref=buffer.at[lax.rem(along + i, 4), h],
            dst_ref=out_recv.at[kind, i - 1, h],
            send_sem=out_send.at[kind, i - 1],
            recv_sem=out_rsem.at[kind, i - 1],
            device_id={"frame": y_peer(i) if kind < 2 else q_peer(i)},
            device_id_type=MESH,
        )

    def out_all(kind, i):
        buffer = (att_send, dq_send, dk_send, dv_send)[kind]
        return pltpu.make_async_remote_copy(
            src_ref=buffer.at[0],
            dst_ref=out_recv.at[kind, i - 1],
            send_sem=out_send.at[kind, i - 1],
            recv_sem=out_rsem.at[kind, i - 1],
            device_id={"frame": y_peer(i) if kind < 2 else q_peer(i)},
            device_id_type=MESH,
        )

    def attend_step(unit, carry):
        h, s = unit // 4, lax.rem(unit, 4)
        cols = pl.ds(pl.multiple_of(h * HD, HD), HD)
        value = allx[V, :, :, cols].reshape(4 * slab, HD)
        summed = dot(probs[unit], value, NN)
        att_send[s, h] = summed.astype(BF16)
        moved = jnp.sum(allx[G, s, :, cols].astype(F32) * summed, axis=1, keepdims=True)
        rows[s] = jnp.where(lane == 16 + h, moved, rows[s])
        return carry

    lax.fori_loop(0, groups * 4, attend_step, 0)

    for s in range(4):
        stats[y, :, s * slab:(s + 1) * slab] = rows[s].T[:24]

    def stat_copy(i):
        return pltpu.make_async_remote_copy(
            src_ref=stats.at[y],
            dst_ref=stats.at[y],
            send_sem=st_send.at[i - 1],
            recv_sem=st_recv.at[i - 1],
            device_id={"frame": y_peer(i)},
            device_id_type=MESH,
        )

    for i in (1, 2, 3):
        stat_copy(i).start()
    for h in range(groups):
        for i in (1, 2, 3):
            out_copy(0, i, h).start()
    for i in (1, 2, 3):
        pltpu.make_async_remote_copy(
            src_ref=stats.at[y],
            dst_ref=stats.at[lax.rem(y + 4 - i, 4)],
            send_sem=st_send.at[i - 1],
            recv_sem=st_recv.at[i - 1],
            device_id={"frame": y_peer(i)},
            device_id_type=MESH,
        ).wait_recv()

    peaks = [stats[d, 0:8, :] for d in range(4)]
    peak = functools.reduce(jnp.maximum, peaks)
    shares = [jnp.exp2(p - peak) for p in peaks]
    total = sum(stats[d, 8:16, :] * shares[d] for d in range(4))
    inverse = 1.0 / total
    delta = sum(stats[d, 16:24, :] * shares[d] for d in range(4)) * inverse
    mine = jnp.exp2(stats[y, 0:8, :] - peak) * inverse
    packed = jnp.concatenate([mine, mine * delta], axis=0)
    packed = jnp.concatenate([packed, jnp.zeros((HD - 16, 4 * slab), F32)], axis=0)
    for s in range(4):
        facts[s] = packed[:, s * slab:(s + 1) * slab].T
    weighted = jnp.concatenate([share * inverse for share in shares], axis=0)
    for s in range(4):

        @pl.when(y == s)
        def _(s=s):
            block = weighted[:, s * slab:(s + 1) * slab]
            block = jnp.concatenate([block, jnp.zeros((HD - 32, slab), F32)], axis=0)
            afacts[...] = block.T

    def pick(block, index):
        return jnp.sum(jnp.where(lane == index, block, 0.0), axis=1, keepdims=True)

    def backward_head(h, carry):
        cols = pl.ds(pl.multiple_of(h * HD, HD), HD)

        def one(s, inner):
            unit = h * 4 + s
            ratio = pick(facts[s], h)
            shift = pick(facts[s], 8 + h)
            grad = (allx[G, s, :, cols].astype(F32) * ratio).astype(BF16)
            scaled[pl.ds(pl.multiple_of(s * slab, slab), slab), :] = grad
            value = allx[V, :, :, cols].reshape(4 * slab, HD)
            key = allx[K, :, :, cols].reshape(4 * slab, HD)
            moved = dot(grad, value, NT)
            score = (probs[unit].astype(F32) * (moved - shift)).astype(BF16)
            grads[pl.ds(pl.multiple_of(s * slab, slab), slab), :] = score
            dq_send[s, h] = (dot(score, key, NN) * scaling).astype(BF16)
            return inner

        lax.fori_loop(0, 4, one, 0)

        def keyside(t, inner):
            span = pl.ds(pl.multiple_of(t * slab, slab), slab)
            weight = probs[pl.ds(h * 4, 4), :, span].reshape(4 * slab, slab)
            dv_send[t, h] = dot(weight, scaled[...], TN).astype(BF16)
            query = allx[Q, :, :, cols].reshape(4 * slab, HD)
            dk_send[t, h] = (dot(grads[:, span], query, TN) * scaling).astype(BF16)
            return inner

        lax.fori_loop(0, 4, keyside, 0)
        for kind in (1, 2, 3):
            for i in (1, 2, 3):
                out_copy(kind, i, h).start()
        return carry

    lax.fori_loop(0, groups, backward_head, 0)

    for i in (1, 2, 3):
        out_all(0, i).wait_recv()

    factor = afacts[...]
    for h in range(groups):
        value = pick(factor, y * 8 + h) * att_send[y, h].astype(F32)
        for i in (1, 2, 3):
            source = lax.rem(y + 4 - i, 4)
            value += pick(factor, source * 8 + h) * out_recv[0, i - 1, h].astype(F32)
        att_out[:, h * HD:(h + 1) * HD] = value.astype(BF16)

    for kind, buffer, out in ((1, dq_send, dq_out), (2, dk_send, dk_out), (3, dv_send, dv_out)):
        for i in (1, 2, 3):
            out_all(kind, i).wait_recv()
        mine_slot = y if kind == 1 else xc
        for h in range(groups):
            value = buffer[mine_slot, h].astype(F32)
            for i in (1, 2, 3):
                value += out_recv[kind, i - 1, h].astype(F32)
            out[:, h * HD:(h + 1) * HD] = value.astype(BF16)

    for a in (Q, K, V, G):
        for d in order[1:]:
            a2a(a, d).wait_send()
        for i in (1, 2, 3):
            slab_copy(a, i).wait_send()
    for i in (1, 2, 3):
        stat_copy(i).wait_send()
        for kind in range(4):
            out_all(kind, i).wait_send()


def local(queries, keys, values, out_grad, tile_mask):
    groups = tile_mask.shape[0]
    nz = lax.axis_size("head")
    slab = queries.shape[0] * nz
    units = groups * 4
    out = jax.ShapeDtypeStruct((slab, groups * HD), BF16)
    hbm = pl.BlockSpec(memory_space=pl.ANY)
    vmem = pl.BlockSpec(memory_space=pltpu.VMEM)
    dma = pltpu.SemaphoreType.DMA
    send = pltpu.VMEM((4, groups, slab, HD), BF16)
    return pl.pallas_call(
        functools.partial(kernel, groups),
        out_shape=(out,) * 4,
        in_specs=[hbm] * 4 + [pl.BlockSpec(memory_space=pltpu.SMEM)],
        out_specs=(vmem,) * 4,
        scratch_shapes=[
            pltpu.VMEM((4, 4, slab, groups * HD), BF16),
            pltpu.VMEM((units, slab, 4 * slab), BF16),
            pltpu.VMEM((4 * slab, 4 * slab), BF16),
            pltpu.VMEM((groups * 8, 8, 8 * TILE), F32),
            pltpu.VMEM((4, slab, HD), F32),
            pltpu.VMEM((4, 24, 4 * slab), F32),
            pltpu.VMEM((4, slab, HD), F32),
            pltpu.VMEM((slab, HD), F32),
            send, send, send, send,
            pltpu.VMEM((4, 3, groups, slab, HD), BF16),
            pltpu.VMEM((4 * slab, HD), BF16),
            dma((4, nz)), dma((4, nz)), dma((4,)), dma((4, 3)), dma((4, 3)),
            dma((3,)), dma((3,)), dma((4, 3)), dma((4, 3)),
        ],
        compiler_params=pltpu.CompilerParams(
            collective_id=0, has_side_effects=True, vmem_limit_bytes=60 << 20
        ),
    )(queries, keys, values, out_grad, tile_mask)


def solution(mesh):
    return jax.shard_map(
        local,
        mesh=mesh,
        in_specs=(
            P(("dp", "frame", "head"), None),
            P(("dp", "frame", "head"), None),
            P(("dp", "frame", "head"), None),
            P(("dp", "frame", "head"), None),
            P("head", None, None),
        ),
        out_specs=(
            P(("dp", "frame"), "head"),
            P(("dp", "frame"), "head"),
            P(("dp", "frame"), "head"),
            P(("dp", "frame"), "head"),
        ),
        check_vma=False,
    )
```

```python
import functools
import math

import jax
import jax.numpy as jnp
from jax import lax
from jax.experimental import pallas as pl
from jax.experimental.pallas import tpu as pltpu
from jax.sharding import PartitionSpec as P

HD = 128
TILE = 128
NEG = -1e30
FLOOR = -1e20
LOG2E = 1.4426950408889634
MESH = pl.DeviceIdType.MESH
F32 = jnp.float32
BF16 = jnp.bfloat16

NT = (((1,), (1,)), ((), ()))
NN = (((1,), (0,)), ((), ()))
TN = (((0,), (0,)), ((), ()))

Q, K, V, G = 0, 1, 2, 3


def dot(a, b, dims):
    return lax.dot_general(a, b, dims, preferred_element_type=F32)


def kernel(
    groups,
    q_hbm, k_hbm, v_hbm, g_hbm, mask_ref,
    att_out, dq_out, dk_out, dv_out,
    allx, probs, grads, bias, rows, stats, deltas, facts, shifts, scaled, parts, halves, landed,
    a2a_send, a2a_recv, own_sem, near_send, near_recv, relay_send, relay_recv,
    st_send, st_recv, dl_send, dl_recv, half_send, half_recv, land_send, land_recv,
):
    z = lax.axis_index("head")
    nz = lax.axis_size("head")
    f = lax.axis_index("frame")
    y, xc = f // 4, lax.rem(f, 4)
    chunk = q_hbm.shape[0]
    slab = chunk * nz
    width = groups * HD
    scaling = 1.0 / math.sqrt(HD)
    c2 = scaling * LOG2E
    inputs = (q_hbm, k_hbm, v_hbm, g_hbm)

    up, down, far = lax.rem(y + 1, 4), lax.rem(y + 3, 4), lax.rem(y + 2, 4)
    core = lax.rem(xc, 2)
    mate = xc + 1 - 2 * core
    across = lax.rem(xc + 2, 4)
    corner = lax.rem(mate + 2, 4)
    y_near = (up * 4 + xc, down * 4 + xc)
    q_near = (y * 4 + mate, y * 4 + across)

    def near(a):
        return y_near if a in (Q, G) else q_near

    def near_slot(a):
        return (up, down) if a in (Q, G) else (mate, across)

    def own_slot(a):
        return y if a in (Q, G) else xc

    def remote(src, dst, send, recv, frame):
        return pltpu.make_async_remote_copy(
            src_ref=src, dst_ref=dst, send_sem=send, recv_sem=recv,
            device_id={"frame": frame}, device_id_type=MESH,
        )

    barrier = pltpu.get_barrier_semaphore()
    for d in range(1, nz):
        pl.semaphore_signal(
            barrier, inc=1, device_id={"head": lax.rem(z + d, nz)}, device_id_type=MESH
        )
    for frame in (*y_near, far * 4 + xc, *q_near):
        pl.semaphore_signal(barrier, inc=1, device_id={"frame": frame}, device_id_type=MESH)
    pl.semaphore_wait(barrier, nz - 1 + 5)

    def a2a(a, d):
        to = lax.rem(z + d, nz)
        return pltpu.make_async_remote_copy(
            src_ref=inputs[a].at[:, pl.ds(pl.multiple_of(to * width, width), width)],
            dst_ref=allx.at[a, own_slot(a), pl.ds(pl.multiple_of(z * chunk, chunk), chunk), :],
            send_sem=a2a_send.at[a, d],
            recv_sem=a2a_recv.at[a, d],
            device_id={"head": to},
            device_id_type=MESH,
        )

    def own(a):
        return pltpu.make_async_copy(
            inputs[a].at[:, pl.ds(pl.multiple_of(z * width, width), width)],
            allx.at[a, own_slot(a), pl.ds(pl.multiple_of(z * chunk, chunk), chunk), :],
            own_sem.at[a],
        )

    def distance(step):
        if isinstance(step, int):
            return (step + 1) // 2 if step % 2 else (nz - step // 2) % nz
        return jnp.where(lax.rem(step, 2) == 1, (step + 1) // 2, lax.rem(nz - step // 2, nz))

    for pair in ((K, Q), (V, G)):
        for a in pair:
            own(a).start()
        for step in range(1, nz):
            for a in pair:
                a2a(a, distance(step)).start()

    def span(d, lo=0, size=None):
        start = lax.rem(z + nz - d, nz) * chunk + lo
        size = chunk if size is None else size
        return pl.ds(pl.multiple_of(start, size), size)

    def near_copy(a, d, i):
        here = allx.at[a, own_slot(a), span(d), :]
        return remote(here, here, near_send.at[a, i], near_recv.at[a, i, d], near(a)[i])

    def near_arrival(a, d, i):
        there = allx.at[a, near_slot(a)[i], span(d), :]
        back = 1 - i if a in (Q, G) else i
        return remote(there, there, near_send.at[a, i], near_recv.at[a, back, d], near(a)[i])

    def relay_copy(a, d, i):
        half = chunk // 2
        if a in (Q, G):
            part = allx.at[a, near_slot(a)[1 - i], span(d, i * half, half), :]
            return remote(part, part, relay_send.at[a, i], relay_recv.at[a, i], near(a)[i])
        part = allx.at[a, across, span(d), :]
        return remote(part, part, relay_send.at[a, 0], relay_recv.at[a, 0], q_near[0])

    def pass_on(a, d, first=False):
        if first:
            own(a).wait()
        else:
            a2a(a, d).wait_recv()
        for i in (0, 1):
            near_copy(a, d, i).start()

    def relay(a, d):
        if a in (Q, G):
            for i in (0, 1):
                near_arrival(a, d, 1 - i).wait_recv()
                relay_copy(a, d, i).start()
        else:
            near_arrival(a, d, 1).wait_recv()
            relay_copy(a, d, 0).start()

    def relay_total(a, i):
        size = slab // 2 if a in (Q, G) else slab
        part = allx.at[a, 0, 0:size, :]
        return remote(part, part, relay_send.at[a, i], relay_recv.at[a, i], near(a)[i])

    def arrived(a):
        if a in (Q, G):
            for i in (0, 1):
                relay_total(a, i).wait_recv()
        else:
            for step in range(nz):
                near_arrival(a, distance(step), 0).wait_recv()
            relay_total(a, 0).wait_recv()

    def bias_row(row, carry):
        h, qt = row // 8, lax.rem(row, 8)
        qi = (qt // 2) * 8 + xc * 2 + lax.rem(qt, 2)
        for kt in range(8):
            live = mask_ref[h, qi, y * 8 + kt]
            value = jnp.where(live == 1, 0.0, NEG).astype(F32)
            bias[row, :, kt * TILE:(kt + 1) * TILE] = jnp.full((8, TILE), value, F32)
        return carry

    for a in (K, Q):
        pass_on(a, 0, True)
    lax.fori_loop(0, groups * 8, bias_row, 0)
    for step in range(1, nz):
        for a in (K, Q):
            pass_on(a, distance(step))
        for a in (K, Q):
            relay(a, distance(step - 1))
    for a in (K, Q):
        relay(a, distance(nz - 1))
    for a in (V, G):
        pass_on(a, 0, True)
    for a in (K, Q):
        arrived(a)

    lane = lax.broadcasted_iota(jnp.int32, (slab, HD), 1)

    def column(h):
        return pl.ds(pl.multiple_of(h * HD, HD), HD)

    def softmax_step(unit):
        h, s = unit // 4, lax.rem(unit, 4)
        cols = column(h)
        query = allx[Q, s, :, cols]
        key = allx[K, :, :, cols].reshape(4 * slab, HD)
        raw = dot(query, key, NT) * c2
        top = raw[:TILE] + bias[h * 8 + 2 * s, 0:1, :]
        low = raw[TILE:] + bias[h * 8 + 2 * s + 1, 0:1, :]
        for part, block in ((0, top), (1, low)):
            peak = jnp.maximum(jnp.max(block, axis=1, keepdims=True), FLOOR)
            weight = jnp.exp2(block - peak)
            total = jnp.sum(weight, axis=1, keepdims=True)
            probs[unit, part * TILE:(part + 1) * TILE, :] = weight.astype(BF16)
            here = pl.ds(part * TILE, TILE)
            old = rows[s, here, :]
            ln = lane[:TILE]
            rows[s, here, :] = jnp.where(ln == h, peak, jnp.where(ln == 8 + h, total, old))

    rows[...] = jnp.zeros_like(rows)

    def travel_step(step, carry):
        for a in (V, G):
            pass_on(a, distance(step))
        for a in (V, G):
            relay(a, distance(step - 1))

        def one(unit, inner):
            softmax_step(unit)
            return inner

        lax.fori_loop(2 * step - 2, 2 * step, one, 0)
        return carry

    lax.fori_loop(1, nz, travel_step, 0)
    for a in (V, G):
        relay(a, distance(nz - 1))

    def rest(unit, carry):
        softmax_step(unit)
        return carry

    lax.fori_loop(2 * nz - 2, groups * 4, rest, 0)

    for s in range(4):
        stats[y, :, s * slab:(s + 1) * slab] = rows[s].T[:16]

    def stat_copy(i, slot):
        frame = (up * 4 + xc, far * 4 + xc, down * 4 + xc)[i]
        part = stats.at[slot]
        return remote(part, part, st_send.at[i], st_recv.at[i], frame)

    def delta_copy(i, slot):
        frame = (up * 4 + xc, far * 4 + xc, down * 4 + xc)[i]
        part = deltas.at[slot]
        return remote(part, part, dl_send.at[i], dl_recv.at[i], frame)

    for i in range(3):
        stat_copy(i, y).start()
    for a in (V, G):
        arrived(a)
    for i in range(3):
        stat_copy(i, (down, far, up)[i]).wait_recv()

    peaks = [stats[d, 0:8, :] for d in range(4)]
    peak = functools.reduce(jnp.maximum, peaks)
    total = sum(stats[d, 8:16, :] * jnp.exp2(peaks[d] - peak) for d in range(4))
    ratio = jnp.exp2(stats[y, 0:8, :] - peak) / total
    blank = jnp.zeros((HD - 8, slab), F32)
    for s in range(4):
        block = jnp.concatenate([ratio[:, s * slab:(s + 1) * slab], blank], axis=0)
        facts[s] = block.T

    def pick(block, index):
        return jnp.sum(jnp.where(lane == index, block, 0.0), axis=1, keepdims=True)

    ATT, DQ, DK, DV = 0, 1, 2, 3

    def half_copies(kind, h):
        half = slab // 2
        if kind in (ATT, DQ):
            return [
                remote(
                    parts.at[kind, far, h, i * half:(i + 1) * half, :],
                    halves.at[kind, h, i * half:(i + 1) * half, :],
                    half_send.at[kind, i], half_recv.at[kind, h, i], y_near[i],
                )
                for i in (0, 1)
            ]
        return [
            remote(
                parts.at[kind, corner, h], halves.at[kind, h],
                half_send.at[kind, 0], half_recv.at[kind, h, 0], q_near[0],
            )
        ]

    def land_copy(kind, h, i):
        slot = (up, down)[i] if kind in (ATT, DQ) else (mate, across)[i]
        frame = y_near[i] if kind in (ATT, DQ) else q_near[i]
        return remote(
            parts.at[kind, slot, h], landed.at[kind, i, h],
            land_send.at[kind, i], land_recv.at[kind, i], frame,
        )

    def first_stage(kind, h):
        for copy in half_copies(kind, h):
            copy.start()
        if kind in (DK, DV):
            land_copy(kind, h, 0).start()

    def second_stage(kind, h):
        half = slab // 2
        for copy in half_copies(kind, h):
            copy.wait_recv()
        if kind in (ATT, DQ):
            for i in (0, 1):
                slot, part = (up, down)[i], slice(i * half, (i + 1) * half)
                mine = parts[kind, slot, h, part, :].astype(F32)
                parts[kind, slot, h, part, :] = (
                    mine + halves[kind, h, part, :].astype(F32)
                ).astype(BF16)
            for i in (0, 1):
                land_copy(kind, h, i).start()
        else:
            mine = parts[kind, across, h].astype(F32)
            parts[kind, across, h] = (mine + halves[kind, h].astype(F32)).astype(BF16)
            land_copy(kind, h, 1).start()

    def attend_head(h, carry):
        cols = column(h)
        value = allx[V, :, :, cols].reshape(4 * slab, HD)
        for s in range(4):
            factor = pick(facts[s], h)
            summed = dot(probs[h * 4 + s], value, NN) * factor
            parts[ATT, s, h] = summed.astype(BF16)
            grad = allx[G, s, :, cols].astype(F32)
            scaled[h, s * slab:(s + 1) * slab, :] = (grad * factor).astype(BF16)
            moved = jnp.sum(grad * summed, axis=1, keepdims=True)
            rows[s] = jnp.where(lane == 16 + h, moved, rows[s])
        first_stage(ATT, h)
        return carry

    lax.fori_loop(0, groups, attend_head, 0)
    for s in range(4):
        deltas[y, :, s * slab:(s + 1) * slab] = rows[s].T[16:24]
    for i in range(3):
        delta_copy(i, y).start()

    def value_head(h, carry):
        turned = scaled[h].T
        weight = probs[pl.ds(h * 4, 4)].reshape(4 * slab, 4 * slab)
        for t in range(4):
            part = dot(turned, weight[:, t * slab:(t + 1) * slab], NN)
            parts[DV, t, h] = part.T.astype(BF16)
        first_stage(DV, h)
        second_stage(ATT, h)
        return carry

    lax.fori_loop(0, groups, value_head, 0)

    for i in range(3):
        delta_copy(i, (down, far, up)[i]).wait_recv()
    delta = sum(deltas[d] for d in range(4)) * ratio
    for s in range(4):
        block = jnp.concatenate([delta[:, s * slab:(s + 1) * slab], blank], axis=0)
        shifts[s] = block.T

    def backward_head(h, carry):
        cols = column(h)

        def one(s, inner):
            here = pl.ds(pl.multiple_of(s * slab, slab), slab)
            shift = pick(shifts[s], h)
            value = allx[V, :, :, cols].reshape(4 * slab, HD)
            key = allx[K, :, :, cols].reshape(4 * slab, HD)
            moved = dot(scaled[h, here, :], value, NT)
            score = (probs[h * 4 + s].astype(F32) * (moved - shift)).astype(BF16)
            grads[here, :] = score
            parts[DQ, s, h] = (dot(score, key, NN) * scaling).astype(BF16)
            return inner

        lax.fori_loop(0, 4, one, 0)
        first_stage(DQ, h)
        query = allx[Q, :, :, cols].reshape(4 * slab, HD)
        turned = query.T
        for t in range(4):
            part = dot(turned, grads[:, t * slab:(t + 1) * slab], NN)
            parts[DK, t, h] = (part.T * scaling).astype(BF16)
        first_stage(DK, h)
        second_stage(DV, h)

        @pl.when(h > 0)
        def _():
            second_stage(DQ, h - 1)
            second_stage(DK, h - 1)

        return carry

    lax.fori_loop(0, groups, backward_head, 0)
    second_stage(DQ, groups - 1)
    second_stage(DK, groups - 1)

    def land_total(kind, i):
        frame = y_near[i] if kind in (ATT, DQ) else q_near[i]
        return remote(
            parts.at[kind, 0], landed.at[kind, i], land_send.at[kind, i], land_recv.at[kind, i], frame
        )

    def land_arrival(kind, i):
        back = 1 - i if kind in (ATT, DQ) else i
        land_total(kind, back).wait_recv()

    for kind, out in ((ATT, att_out), (DV, dv_out), (DK, dk_out), (DQ, dq_out)):
        for i in (0, 1):
            land_arrival(kind, i)
        slot = y if kind in (ATT, DQ) else xc
        for h in range(groups):
            value = parts[kind, slot, h].astype(F32)
            for i in (0, 1):
                value += landed[kind, i, h].astype(F32)
            out[:, h * HD:(h + 1) * HD] = value.astype(BF16)

    for a in (Q, K, V, G):
        for d in range(1, nz):
            a2a(a, d).wait_send()
        for i in (0, 1):
            part = allx.at[a, 0]
            remote(part, part, near_send.at[a, i], relay_recv.at[a, 0], near(a)[i]).wait_send()
        for i in (0, 1) if a in (Q, G) else (0,):
            relay_total(a, i).wait_send()
    for i in range(3):
        stat_copy(i, y).wait_send()
        delta_copy(i, y).wait_send()
    for kind in range(4):
        for i in (0, 1) if kind in (ATT, DQ) else (0,):
            size = slab // 2 if kind in (ATT, DQ) else slab
            part = parts.at[kind, 0, :, 0:size, :]
            remote(
                part, part, half_send.at[kind, i], half_recv.at[kind, 0, i], y_near[i]
            ).wait_send()
        for i in (0, 1):
            land_total(kind, i).wait_send()


def local(queries, keys, values, out_grad, tile_mask):
    groups = tile_mask.shape[0]
    nz = lax.axis_size("head")
    slab = queries.shape[0] * nz
    units = groups * 4
    out = jax.ShapeDtypeStruct((slab, groups * HD), BF16)
    hbm = pl.BlockSpec(memory_space=pl.ANY)
    vmem = pl.BlockSpec(memory_space=pltpu.VMEM)
    dma = pltpu.SemaphoreType.DMA
    return pl.pallas_call(
        functools.partial(kernel, groups),
        out_shape=(out,) * 4,
        in_specs=[hbm] * 4 + [pl.BlockSpec(memory_space=pltpu.SMEM)],
        out_specs=(vmem,) * 4,
        scratch_shapes=[
            pltpu.VMEM((4, 4, slab, groups * HD), BF16),
            pltpu.VMEM((units, slab, 4 * slab), BF16),
            pltpu.VMEM((4 * slab, 4 * slab), BF16),
            pltpu.VMEM((groups * 8, 8, 8 * TILE), F32),
            pltpu.VMEM((4, slab, HD), F32),
            pltpu.VMEM((4, 16, 4 * slab), F32),
            pltpu.VMEM((4, 8, 4 * slab), F32),
            pltpu.VMEM((4, slab, HD), F32),
            pltpu.VMEM((4, slab, HD), F32),
            pltpu.VMEM((groups, 4 * slab, HD), BF16),
            pltpu.VMEM((4, 4, groups, slab, HD), BF16),
            pltpu.VMEM((4, groups, slab, HD), BF16),
            pltpu.VMEM((4, 2, groups, slab, HD), BF16),
            dma((4, nz)), dma((4, nz)), dma((4,)), dma((4, 2)), dma((4, 2, nz)),
            dma((4, 2)), dma((4, 2)), dma((3,)), dma((3,)), dma((3,)), dma((3,)),
            dma((4, 2)), dma((4, groups, 2)), dma((4, 2)), dma((4, 2)),
        ],
        compiler_params=pltpu.CompilerParams(
            collective_id=0, has_side_effects=True, vmem_limit_bytes=56 << 20
        ),
    )(queries, keys, values, out_grad, tile_mask)


def solution(mesh):
    return jax.shard_map(
        local,
        mesh=mesh,
        in_specs=(
            P(("dp", "frame", "head"), None),
            P(("dp", "frame", "head"), None),
            P(("dp", "frame", "head"), None),
            P(("dp", "frame", "head"), None),
            P("head", None, None),
        ),
        out_specs=(
            P(("dp", "frame"), "head"),
            P(("dp", "frame"), "head"),
            P(("dp", "frame"), "head"),
            P(("dp", "frame"), "head"),
        ),
        check_vma=False,
    )
```

```python
import functools
import math

import jax
import jax.numpy as jnp
from jax import lax
from jax.experimental import pallas as pl
from jax.experimental.pallas import tpu as pltpu
from jax.sharding import PartitionSpec as P

HD = 128
TILE = 128
NEG = -1e30
FLOOR = -1e20
LOG2E = 1.4426950408889634
MESH = pl.DeviceIdType.MESH
F32 = jnp.float32
BF16 = jnp.bfloat16

NT = (((1,), (1,)), ((), ()))
NN = (((1,), (0,)), ((), ()))
TN = (((0,), (0,)), ((), ()))

Q, K, V, G = 0, 1, 2, 3


def dot(a, b, dims):
    return lax.dot_general(a, b, dims, preferred_element_type=F32)


def kernel(
    groups,
    q_hbm, k_hbm, v_hbm, g_hbm, mask_ref,
    att_out, dq_out, dk_out, dv_out,
    allx, probs, grads, bias, rows, stats, deltas, facts, shifts, scaled, parts, halves, landed,
    a2a_send, a2a_recv, own_sem, near_send, near_recv,
    st_send, st_recv, dl_send, dl_recv, half_send, half_recv, land_send, land_recv,
):
    z = lax.axis_index("head")
    nz = lax.axis_size("head")
    f = lax.axis_index("frame")
    y, xc = f // 4, lax.rem(f, 4)
    chunk = q_hbm.shape[0]
    slab = chunk * nz
    width = groups * HD
    scaling = 1.0 / math.sqrt(HD)
    c2 = scaling * LOG2E
    inputs = (q_hbm, k_hbm, v_hbm, g_hbm)

    up, down, far = lax.rem(y + 1, 4), lax.rem(y + 3, 4), lax.rem(y + 2, 4)
    core = lax.rem(xc, 2)
    mate = xc + 1 - 2 * core
    across = lax.rem(xc + 2, 4)
    corner = lax.rem(mate + 2, 4)
    y_near = (up * 4 + xc, down * 4 + xc)
    q_near = (y * 4 + mate, y * 4 + across)

    def own_slot(a):
        return y if a in (Q, G) else xc

    def remote(src, dst, send, recv, frame):
        return pltpu.make_async_remote_copy(
            src_ref=src, dst_ref=dst, send_sem=send, recv_sem=recv,
            device_id={"frame": frame}, device_id_type=MESH,
        )

    barrier = pltpu.get_barrier_semaphore()
    for d in range(1, nz):
        pl.semaphore_signal(
            barrier, inc=1, device_id={"head": lax.rem(z + d, nz)}, device_id_type=MESH
        )
    for frame in (*y_near, far * 4 + xc, *q_near, y * 4 + corner):
        pl.semaphore_signal(barrier, inc=1, device_id={"frame": frame}, device_id_type=MESH)
    pl.semaphore_wait(barrier, nz - 1 + 6)

    def a2a(a, d):
        to = lax.rem(z + d, nz)
        return pltpu.make_async_remote_copy(
            src_ref=inputs[a].at[:, pl.ds(pl.multiple_of(to * width, width), width)],
            dst_ref=allx.at[a, own_slot(a), pl.ds(pl.multiple_of(z * chunk, chunk), chunk), :],
            send_sem=a2a_send.at[a, d],
            recv_sem=a2a_recv.at[a, d],
            device_id={"head": to},
            device_id_type=MESH,
        )

    def own(a):
        return pltpu.make_async_copy(
            inputs[a].at[:, pl.ds(pl.multiple_of(z * width, width), width)],
            allx.at[a, own_slot(a), pl.ds(pl.multiple_of(z * chunk, chunk), chunk), :],
            own_sem.at[a],
        )

    def distance(step):
        if isinstance(step, int):
            return (step + 1) // 2 if step % 2 else (nz - step // 2) % nz
        return jnp.where(lax.rem(step, 2) == 1, (step + 1) // 2, lax.rem(nz - step // 2, nz))

    for pair in ((K, Q), (V, G)):
        for a in pair:
            own(a).start()
        for step in range(1, nz):
            for a in pair:
                a2a(a, distance(step)).start()

    def span(d, lo=0, size=None):
        start = lax.rem(z + nz - d, nz) * chunk + lo
        size = chunk if size is None else size
        return pl.ds(pl.multiple_of(start, size), size)

    def partner(a, i):
        if a in (Q, G):
            return (up, down, far)[i] * 4 + xc
        return y * 4 + (mate, across, corner)[i]

    def pass_on(a, d, first=False):
        if first:
            own(a).wait()
        else:
            a2a(a, d).wait_recv()
        here = allx.at[a, own_slot(a), span(d), :]
        for i in (2, 0, 1):
            remote(here, here, near_send.at[a, i], near_recv.at[a, i], partner(a, i)).start()

    def slab_total(a, i):
        part = allx.at[a, own_slot(a)]
        return remote(part, part, near_send.at[a, i], near_recv.at[a, i], partner(a, i))

    def arrived(a):
        for i in (0, 1, 2):
            slab_total(a, i).wait_recv()

    def bias_row(row, carry):
        h, qt = row // 8, lax.rem(row, 8)
        qi = (qt // 2) * 8 + xc * 2 + lax.rem(qt, 2)
        for kt in range(8):
            live = mask_ref[h, qi, y * 8 + kt]
            value = jnp.where(live == 1, 0.0, NEG).astype(F32)
            bias[row, :, kt * TILE:(kt + 1) * TILE] = jnp.full((8, TILE), value, F32)
        return carry

    for a in (K, Q, V, G):
        pass_on(a, 0, True)
    lax.fori_loop(0, groups * 8, bias_row, 0)
    for step in range(1, nz):
        for a in (K, Q):
            pass_on(a, distance(step))
    for a in (K, Q):
        arrived(a)

    lane = lax.broadcasted_iota(jnp.int32, (slab, HD), 1)

    def column(h):
        return pl.ds(pl.multiple_of(h * HD, HD), HD)

    def softmax_step(unit):
        h, s = unit // 4, lax.rem(unit, 4)
        cols = column(h)
        query = allx[Q, s, :, cols]
        key = allx[K, :, :, cols].reshape(4 * slab, HD)
        raw = dot(query, key, NT) * c2
        top = raw[:TILE] + bias[h * 8 + 2 * s, 0:1, :]
        low = raw[TILE:] + bias[h * 8 + 2 * s + 1, 0:1, :]
        for part, block in ((0, top), (1, low)):
            peak = jnp.maximum(jnp.max(block, axis=1, keepdims=True), FLOOR)
            weight = jnp.exp2(block - peak)
            total = jnp.sum(weight, axis=1, keepdims=True)
            probs[unit, part * TILE:(part + 1) * TILE, :] = weight.astype(BF16)
            here = pl.ds(part * TILE, TILE)
            old = rows[s, here, :]
            ln = lane[:TILE]
            rows[s, here, :] = jnp.where(ln == h, peak, jnp.where(ln == 8 + h, total, old))

    rows[...] = jnp.zeros_like(rows)

    def stat_copy(i, slot):
        frame = (up * 4 + xc, far * 4 + xc, down * 4 + xc)[i]
        part = stats.at[slot]
        return remote(part, part, st_send.at[i], st_recv.at[i], frame)

    def share_stats():
        for s in range(4):
            stats[y, :, s * slab:(s + 1) * slab] = rows[s].T[:16]
        for i in range(3):
            stat_copy(i, y).start()

    def one_unit(unit, carry):
        softmax_step(unit)
        return carry

    units = groups * 4
    done = 0
    for step in range(1, nz):
        for a in (V, G):
            pass_on(a, distance(step))
        if step % 2 == 0:
            until = units if step >= nz - 2 else min(units, done + (6 if step == 2 else 9))
            lax.fori_loop(done, until, one_unit, 0)
            done = until
        if step == nz - 2:
            share_stats()

    def delta_copy(i, slot):
        frame = (up * 4 + xc, far * 4 + xc, down * 4 + xc)[i]
        part = deltas.at[slot]
        return remote(part, part, dl_send.at[i], dl_recv.at[i], frame)

    for i in range(3):
        stat_copy(i, (down, far, up)[i]).wait_recv()

    peaks = [stats[d, 0:8, :] for d in range(4)]
    peak = functools.reduce(jnp.maximum, peaks)
    total = sum(stats[d, 8:16, :] * jnp.exp2(peaks[d] - peak) for d in range(4))
    ratio = jnp.exp2(stats[y, 0:8, :] - peak) / total
    blank = jnp.zeros((HD - 8, slab), F32)
    for s in range(4):
        block = jnp.concatenate([ratio[:, s * slab:(s + 1) * slab], blank], axis=0)
        facts[s] = block.T

    def pick(block, index):
        return jnp.sum(jnp.where(lane == index, block, 0.0), axis=1, keepdims=True)

    ATT, DQ, DK, DV = 0, 1, 2, 3

    def half_copies(kind, h):
        half = slab // 2
        if kind in (ATT, DQ):
            return [
                remote(
                    parts.at[kind, far, h, i * half:(i + 1) * half, :],
                    halves.at[kind, h, i * half:(i + 1) * half, :],
                    half_send.at[kind, i], half_recv.at[kind, h, i], y_near[i],
                )
                for i in (0, 1)
            ]
        return [
            remote(
                parts.at[kind, corner, h], halves.at[kind, h],
                half_send.at[kind, 0], half_recv.at[kind, h, 0], q_near[0],
            )
        ]

    def land_copy(kind, h, i):
        slot = (up, down)[i] if kind in (ATT, DQ) else (mate, across)[i]
        frame = y_near[i] if kind in (ATT, DQ) else q_near[i]
        return remote(
            parts.at[kind, slot, h], landed.at[kind, i, h],
            land_send.at[kind, i], land_recv.at[kind, i], frame,
        )

    def first_stage(kind, h):
        for copy in half_copies(kind, h):
            copy.start()
        if kind in (DK, DV):
            land_copy(kind, h, 0).start()

    def second_stage(kind, h):
        half = slab // 2
        for copy in half_copies(kind, h):
            copy.wait_recv()
        if kind in (ATT, DQ):
            for i in (0, 1):
                slot, part = (up, down)[i], slice(i * half, (i + 1) * half)
                mine = parts[kind, slot, h, part, :].astype(F32)
                parts[kind, slot, h, part, :] = (
                    mine + halves[kind, h, part, :].astype(F32)
                ).astype(BF16)
            for i in (0, 1):
                land_copy(kind, h, i).start()
        else:
            mine = parts[kind, across, h].astype(F32)
            parts[kind, across, h] = (mine + halves[kind, h].astype(F32)).astype(BF16)
            land_copy(kind, h, 1).start()

    for a in (V, G):
        arrived(a)

    def attend_head(h, carry):
        cols = column(h)
        value = allx[V, :, :, cols].reshape(4 * slab, HD)
        for s in range(4):
            factor = pick(facts[s], h)
            summed = dot(probs[h * 4 + s], value, NN) * factor
            parts[ATT, s, h] = summed.astype(BF16)
            grad = allx[G, s, :, cols].astype(F32)
            scaled[h, s * slab:(s + 1) * slab, :] = (grad * factor).astype(BF16)
            moved = jnp.sum(grad * summed, axis=1, keepdims=True)
            rows[s] = jnp.where(lane == 16 + h, moved, rows[s])
        first_stage(ATT, h)
        return carry

    lax.fori_loop(0, groups, attend_head, 0)
    for s in range(4):
        deltas[y, :, s * slab:(s + 1) * slab] = rows[s].T[16:24]
    for i in range(3):
        delta_copy(i, y).start()

    def value_head(h, carry):
        turned = scaled[h].T
        weight = probs[pl.ds(h * 4, 4)].reshape(4 * slab, 4 * slab)
        for t in range(4):
            part = dot(turned, weight[:, t * slab:(t + 1) * slab], NN)
            parts[DV, t, h] = part.T.astype(BF16)
        first_stage(DV, h)
        second_stage(ATT, h)
        return carry

    lax.fori_loop(0, groups, value_head, 0)

    for i in range(3):
        delta_copy(i, (down, far, up)[i]).wait_recv()
    delta = sum(deltas[d] for d in range(4)) * ratio
    for s in range(4):
        block = jnp.concatenate([delta[:, s * slab:(s + 1) * slab], blank], axis=0)
        shifts[s] = block.T

    def backward_head(h, carry):
        cols = column(h)

        def one(s, inner):
            here = pl.ds(pl.multiple_of(s * slab, slab), slab)
            shift = pick(shifts[s], h)
            value = allx[V, :, :, cols].reshape(4 * slab, HD)
            key = allx[K, :, :, cols].reshape(4 * slab, HD)
            moved = dot(scaled[h, here, :], value, NT)
            score = (probs[h * 4 + s].astype(F32) * (moved - shift)).astype(BF16)
            grads[here, :] = score
            parts[DQ, s, h] = (dot(score, key, NN) * scaling).astype(BF16)
            return inner

        lax.fori_loop(0, 4, one, 0)
        first_stage(DQ, h)
        query = allx[Q, :, :, cols].reshape(4 * slab, HD)
        turned = query.T
        for t in range(4):
            part = dot(turned, grads[:, t * slab:(t + 1) * slab], NN)
            parts[DK, t, h] = (part.T * scaling).astype(BF16)
        first_stage(DK, h)
        second_stage(DV, h)

        @pl.when(h > 0)
        def _():
            second_stage(DQ, h - 1)
            second_stage(DK, h - 1)

        return carry

    lax.fori_loop(0, groups, backward_head, 0)
    second_stage(DQ, groups - 1)
    second_stage(DK, groups - 1)

    def land_total(kind, i):
        frame = y_near[i] if kind in (ATT, DQ) else q_near[i]
        return remote(
            parts.at[kind, 0], landed.at[kind, i], land_send.at[kind, i], land_recv.at[kind, i], frame
        )

    def land_arrival(kind, i):
        back = 1 - i if kind in (ATT, DQ) else i
        land_total(kind, back).wait_recv()

    for kind, out in ((ATT, att_out), (DV, dv_out), (DK, dk_out), (DQ, dq_out)):
        for i in (0, 1):
            land_arrival(kind, i)
        slot = y if kind in (ATT, DQ) else xc
        for h in range(groups):
            value = parts[kind, slot, h].astype(F32)
            for i in (0, 1):
                value += landed[kind, i, h].astype(F32)
            out[:, h * HD:(h + 1) * HD] = value.astype(BF16)

    for a in (Q, K, V, G):
        for d in range(1, nz):
            a2a(a, d).wait_send()
        for i in (0, 1, 2):
            slab_total(a, i).wait_send()
    for i in range(3):
        stat_copy(i, y).wait_send()
        delta_copy(i, y).wait_send()
    for kind in range(4):
        for i in (0, 1) if kind in (ATT, DQ) else (0,):
            size = slab // 2 if kind in (ATT, DQ) else slab
            part = parts.at[kind, 0, :, 0:size, :]
            remote(
                part, part, half_send.at[kind, i], half_recv.at[kind, 0, i], y_near[i]
            ).wait_send()
        for i in (0, 1):
            land_total(kind, i).wait_send()


def local(queries, keys, values, out_grad, tile_mask):
    groups = tile_mask.shape[0]
    nz = lax.axis_size("head")
    slab = queries.shape[0] * nz
    units = groups * 4
    out = jax.ShapeDtypeStruct((slab, groups * HD), BF16)
    hbm = pl.BlockSpec(memory_space=pl.ANY)
    vmem = pl.BlockSpec(memory_space=pltpu.VMEM)
    dma = pltpu.SemaphoreType.DMA
    return pl.pallas_call(
        functools.partial(kernel, groups),
        out_shape=(out,) * 4,
        in_specs=[hbm] * 4 + [pl.BlockSpec(memory_space=pltpu.SMEM)],
        out_specs=(vmem,) * 4,
        scratch_shapes=[
            pltpu.VMEM((4, 4, slab, groups * HD), BF16),
            pltpu.VMEM((units, slab, 4 * slab), BF16),
            pltpu.VMEM((4 * slab, 4 * slab), BF16),
            pltpu.VMEM((groups * 8, 8, 8 * TILE), F32),
            pltpu.VMEM((4, slab, HD), F32),
            pltpu.VMEM((4, 16, 4 * slab), F32),
            pltpu.VMEM((4, 8, 4 * slab), F32),
            pltpu.VMEM((4, slab, HD), F32),
            pltpu.VMEM((4, slab, HD), F32),
            pltpu.VMEM((groups, 4 * slab, HD), BF16),
            pltpu.VMEM((4, 4, groups, slab, HD), BF16),
            pltpu.VMEM((4, groups, slab, HD), BF16),
            pltpu.VMEM((4, 2, groups, slab, HD), BF16),
            dma((4, nz)), dma((4, nz)), dma((4,)), dma((4, 3)), dma((4, 3)),
            dma((3,)), dma((3,)), dma((3,)), dma((3,)),
            dma((4, 2)), dma((4, groups, 2)), dma((4, 2)), dma((4, 2)),
        ],
        compiler_params=pltpu.CompilerParams(
            collective_id=0, has_side_effects=True, vmem_limit_bytes=56 << 20
        ),
    )(queries, keys, values, out_grad, tile_mask)


def solution(mesh):
    return jax.shard_map(
        local,
        mesh=mesh,
        in_specs=(
            P(("dp", "frame", "head"), None),
            P(("dp", "frame", "head"), None),
            P(("dp", "frame", "head"), None),
            P(("dp", "frame", "head"), None),
            P("head", None, None),
        ),
        out_specs=(
            P(("dp", "frame"), "head"),
            P(("dp", "frame"), "head"),
            P(("dp", "frame"), "head"),
            P(("dp", "frame"), "head"),
        ),
        check_vma=False,
    )
```

```python
import functools
import math

import jax
import jax.numpy as jnp
from jax import lax
from jax.experimental import pallas as pl
from jax.experimental.pallas import tpu as pltpu
from jax.sharding import PartitionSpec as P

HD = 128
TILE = 128
NEG = -1e30
S2, S4, S6 = 2, 9, 6
FLOOR = -1e20
LOG2E = 1.4426950408889634
MESH = pl.DeviceIdType.MESH
F32 = jnp.float32
BF16 = jnp.bfloat16

NT = (((1,), (1,)), ((), ()))
NN = (((1,), (0,)), ((), ()))
TN = (((0,), (0,)), ((), ()))

Q, K, V, G = 0, 1, 2, 3


def dot(a, b, dims):
    return lax.dot_general(a, b, dims, preferred_element_type=F32)


def kernel(
    groups,
    q_hbm, k_hbm, v_hbm, g_hbm, mask_hbm,
    att_out, dq_out, dk_out, dv_out,
    mask_ref, allx, probs, bias, rows, stats, deltas, facts, shifts, scaled, parts, halves, landed, results,
    result_sem,
    mask_sem, a2a_send, a2a_recv, own_sem, near_send, near_recv,
    st_send, st_recv, dl_send, dl_recv, half_send, half_recv, land_send, land_recv,
):
    z = lax.axis_index("head")
    nz = lax.axis_size("head")
    f = lax.axis_index("frame")
    y, xc = f // 4, lax.rem(f, 4)
    chunk = q_hbm.shape[0]
    slab = chunk * nz
    width = groups * HD
    scaling = 1.0 / math.sqrt(HD)
    c2 = scaling * LOG2E
    inputs = (q_hbm, k_hbm, v_hbm, g_hbm)

    up, down, far = lax.rem(y + 1, 4), lax.rem(y + 3, 4), lax.rem(y + 2, 4)
    core = lax.rem(xc, 2)
    mate = xc + 1 - 2 * core
    across = lax.rem(xc + 2, 4)
    corner = lax.rem(mate + 2, 4)
    y_near = (up * 4 + xc, down * 4 + xc)
    q_near = (y * 4 + mate, y * 4 + across)

    def own_slot(a):
        return y if a in (Q, G) else xc

    def remote(src, dst, send, recv, frame):
        return pltpu.make_async_remote_copy(
            src_ref=src, dst_ref=dst, send_sem=send, recv_sem=recv,
            device_id={"frame": frame}, device_id_type=MESH,
        )

    mask_copy = pltpu.make_async_copy(mask_hbm, mask_ref, mask_sem)
    mask_copy.start()
    barrier = pltpu.get_barrier_semaphore()
    for d in range(1, nz):
        pl.semaphore_signal(
            barrier, inc=1, device_id={"head": lax.rem(z + d, nz)}, device_id_type=MESH
        )
    for frame in (*y_near, far * 4 + xc, *q_near, y * 4 + corner):
        pl.semaphore_signal(barrier, inc=1, device_id={"frame": frame}, device_id_type=MESH)
    pl.semaphore_wait(barrier, nz - 1 + 6)

    def a2a(a, d):
        to = lax.rem(z + d, nz)
        return pltpu.make_async_remote_copy(
            src_ref=inputs[a].at[:, pl.ds(pl.multiple_of(to * width, width), width)],
            dst_ref=allx.at[a, own_slot(a), pl.ds(pl.multiple_of(z * chunk, chunk), chunk), :],
            send_sem=a2a_send.at[a, d],
            recv_sem=a2a_recv.at[a, d],
            device_id={"head": to},
            device_id_type=MESH,
        )

    def own(a):
        return pltpu.make_async_copy(
            inputs[a].at[:, pl.ds(pl.multiple_of(z * width, width), width)],
            allx.at[a, own_slot(a), pl.ds(pl.multiple_of(z * chunk, chunk), chunk), :],
            own_sem.at[a],
        )

    def distance(step):
        if isinstance(step, int):
            return (step + 1) // 2 if step % 2 else (nz - step // 2) % nz
        return jnp.where(lax.rem(step, 2) == 1, (step + 1) // 2, lax.rem(nz - step // 2, nz))

    for pair in ((K, Q), (V, G)):
        for a in pair:
            own(a).start()
        for step in range(1, nz):
            for a in pair:
                a2a(a, distance(step)).start()

    def span(d, lo=0, size=None):
        start = lax.rem(z + nz - d, nz) * chunk + lo
        size = chunk if size is None else size
        return pl.ds(pl.multiple_of(start, size), size)

    def partner(a, i):
        if a in (Q, G):
            return (up, down, far)[i] * 4 + xc
        return y * 4 + (mate, across, corner)[i]

    def pass_on(a, d, first=False):
        if first:
            own(a).wait()
        else:
            a2a(a, d).wait_recv()
        here = allx.at[a, own_slot(a), span(d), :]
        for i in (2, 0, 1):
            remote(here, here, near_send.at[a, i], near_recv.at[a, i], partner(a, i)).start()

    def slab_total(a, i):
        part = allx.at[a, own_slot(a)]
        return remote(part, part, near_send.at[a, i], near_recv.at[a, i], partner(a, i))

    def arrived(a):
        for i in (0, 1, 2):
            slab_total(a, i).wait_recv()

    def bias_row(row, carry):
        h, qt = row // 8, lax.rem(row, 8)
        qi = (qt // 2) * 8 + xc * 2 + lax.rem(qt, 2)
        for kt in range(8):
            live = mask_ref[h, qi, y * 8 + kt]
            value = jnp.where(live == 1, 0.0, NEG).astype(F32)
            bias[row, :, kt * TILE:(kt + 1) * TILE] = jnp.full((8, TILE), value, F32)
        return carry

    for a in (K, Q, V, G):
        pass_on(a, 0, True)
    mask_copy.wait()
    lax.fori_loop(0, groups * 8, bias_row, 0)
    for step in range(1, nz):
        for a in (K, Q):
            pass_on(a, distance(step))
    lane = lax.broadcasted_iota(jnp.int32, (slab, HD), 1)

    def column(h):
        return pl.ds(pl.multiple_of(h * HD, HD), HD)

    def softmax_step(unit):
        h, s = unit // 4, lax.rem(unit, 4)
        cols = column(h)
        query = allx[Q, s, :, cols]
        key = allx[K, :, :, cols].reshape(4 * slab, HD)
        raw = dot(query, key, NT) * c2
        top = raw[:TILE] + bias[h * 8 + 2 * s, 0:1, :]
        low = raw[TILE:] + bias[h * 8 + 2 * s + 1, 0:1, :]
        for part, block in ((0, top), (1, low)):
            peak = jnp.maximum(jnp.max(block, axis=1, keepdims=True), FLOOR)
            weight = jnp.exp2(block - peak)
            total = jnp.sum(weight, axis=1, keepdims=True)
            probs[unit, part * TILE:(part + 1) * TILE, :] = weight.astype(BF16)
            here = pl.ds(part * TILE, TILE)
            old = rows[s, here, :]
            ln = lane[:TILE]
            rows[s, here, :] = jnp.where(ln == h, peak, jnp.where(ln == 8 + h, total, old))

    rows[...] = jnp.zeros_like(rows)

    def stat_copy(i, slot):
        frame = (up * 4 + xc, far * 4 + xc, down * 4 + xc)[i]
        part = stats.at[slot]
        return remote(part, part, st_send.at[i], st_recv.at[i], frame)

    def share_stats():
        for s in range(4):
            stats[y, :, s * slab:(s + 1) * slab] = rows[s].T[:16]
        for i in range(3):
            stat_copy(i, y).start()

    def one_unit(unit, carry):
        softmax_step(unit)
        return carry

    units = groups * 4
    done = 0
    for step in range(1, nz):
        for a in (V, G):
            pass_on(a, distance(step))
        if step == 2:
            for a in (K, Q):
                arrived(a)
        if step % 2 == 0 or step == nz - 1:
            until = units if step == nz - 1 else min(units, done + {2: S2, 4: S4, 6: S6}.get(step, 0))
            lax.fori_loop(done, until, one_unit, 0)
            done = until
    share_stats()

    def delta_copy(i, slot):
        frame = (up * 4 + xc, far * 4 + xc, down * 4 + xc)[i]
        part = deltas.at[slot]
        return remote(part, part, dl_send.at[i], dl_recv.at[i], frame)

    for i in range(3):
        stat_copy(i, (down, far, up)[i]).wait_recv()

    peaks = [stats[d, 0:8, :] for d in range(4)]
    peak = functools.reduce(jnp.maximum, peaks)
    total = sum(stats[d, 8:16, :] * jnp.exp2(peaks[d] - peak) for d in range(4))
    ratio = jnp.exp2(stats[y, 0:8, :] - peak) / total
    blank = jnp.zeros((HD - 8, slab), F32)
    for s in range(4):
        block = jnp.concatenate([ratio[:, s * slab:(s + 1) * slab], blank], axis=0)
        facts[s] = block.T

    def pick(block, index):
        return jnp.sum(jnp.where(lane == index, block, 0.0), axis=1, keepdims=True)

    ATT, DQ, DK, DV = 0, 1, 2, 3

    def half_copies(kind, h):
        half = slab // 2
        if kind in (ATT, DQ):
            return [
                remote(
                    parts.at[kind, far, h, i * half:(i + 1) * half, :],
                    halves.at[kind, h, i * half:(i + 1) * half, :],
                    half_send.at[kind, i], half_recv.at[kind, h, i], y_near[i],
                )
                for i in (0, 1)
            ]
        return [
            remote(
                parts.at[kind, corner, h], halves.at[kind, h],
                half_send.at[kind, 0], half_recv.at[kind, h, 0], q_near[0],
            )
        ]

    def land_copy(kind, h, i):
        slot = (up, down)[i] if kind in (ATT, DQ) else (mate, across)[i]
        frame = y_near[i] if kind in (ATT, DQ) else q_near[i]
        return remote(
            parts.at[kind, slot, h], landed.at[kind, i, h],
            land_send.at[kind, i], land_recv.at[kind, i], frame,
        )

    def first_stage(kind, h):
        for copy in half_copies(kind, h):
            copy.start()
        if kind in (DK, DV):
            land_copy(kind, h, 0).start()

    def second_stage(kind, h):
        half = slab // 2
        for copy in half_copies(kind, h):
            copy.wait_recv()
        if kind in (ATT, DQ):
            for i in (0, 1):
                slot, part = (up, down)[i], slice(i * half, (i + 1) * half)
                mine = parts[kind, slot, h, part, :].astype(F32)
                parts[kind, slot, h, part, :] = (
                    mine + halves[kind, h, part, :].astype(F32)
                ).astype(BF16)
            for i in (0, 1):
                land_copy(kind, h, i).start()
        else:
            mine = parts[kind, across, h].astype(F32)
            parts[kind, across, h] = (mine + halves[kind, h].astype(F32)).astype(BF16)
            land_copy(kind, h, 1).start()

    for a in (V, G):
        arrived(a)

    def attend_head(h, carry):
        cols = column(h)
        value = allx[V, :, :, cols].reshape(4 * slab, HD)
        for s in range(4):
            factor = pick(facts[s], h)
            summed = dot(probs[h * 4 + s], value, NN) * factor
            parts[ATT, s, h] = summed.astype(BF16)
            grad = allx[G, s, :, cols].astype(F32)
            scaled[h, s * slab:(s + 1) * slab, :] = (grad * factor).astype(BF16)
            moved = jnp.sum(grad * summed, axis=1, keepdims=True)
            rows[s] = jnp.where(lane == 16 + h, moved, rows[s])
        first_stage(ATT, h)
        return carry

    lax.fori_loop(0, groups, attend_head, 0)
    for s in range(4):
        deltas[y, :, s * slab:(s + 1) * slab] = rows[s].T[16:24]
    for i in range(3):
        delta_copy(i, y).start()

    def value_head(h, carry):
        turned = scaled[h].T
        weight = probs[pl.ds(h * 4, 4)].reshape(4 * slab, 4 * slab)
        for t in range(4):
            part = dot(turned, weight[:, t * slab:(t + 1) * slab], NN)
            parts[DV, t, h] = part.T.astype(BF16)
        first_stage(DV, h)
        second_stage(ATT, h)
        return carry

    lax.fori_loop(0, groups, value_head, 0)

    for i in range(3):
        delta_copy(i, (down, far, up)[i]).wait_recv()
    delta = sum(deltas[d] for d in range(4)) * ratio
    for s in range(4):
        block = jnp.concatenate([delta[:, s * slab:(s + 1) * slab], blank], axis=0)
        shifts[s] = block.T

    def query_head(h, carry):
        cols = column(h)

        value = allx[V, :, :, cols].reshape(4 * slab, HD)
        key = allx[K, :, :, cols].reshape(4 * slab, HD)
        for s in range(4):
            shift = pick(shifts[s], h)
            moved = dot(scaled[h, s * slab:(s + 1) * slab, :], value, NT)
            score = (probs[h * 4 + s].astype(F32) * (moved - shift)).astype(BF16)
            probs[h * 4 + s] = score
            parts[DQ, s, h] = (dot(score, key, NN) * scaling).astype(BF16)
        first_stage(DQ, h)
        second_stage(DV, h)
        return carry

    lax.fori_loop(0, groups, query_head, 0)

    def key_head(h, carry):
        turned = allx[Q, :, :, column(h)].reshape(4 * slab, HD).T
        score = probs[pl.ds(h * 4, 4)].reshape(4 * slab, 4 * slab)
        for t in range(4):
            part = dot(turned, score[:, t * slab:(t + 1) * slab], NN)
            parts[DK, t, h] = (part.T * scaling).astype(BF16)
        first_stage(DK, h)
        second_stage(DQ, h)

        @pl.when(h > 0)
        def _():
            second_stage(DK, h - 1)

        return carry

    lax.fori_loop(0, groups, key_head, 0)

    def land_total(kind, i):
        frame = y_near[i] if kind in (ATT, DQ) else q_near[i]
        return remote(
            parts.at[kind, 0], landed.at[kind, i], land_send.at[kind, i], land_recv.at[kind, i], frame
        )

    def land_arrival(kind, i):
        back = 1 - i if kind in (ATT, DQ) else i
        land_total(kind, back).wait_recv()

    def finish(kind, out):
        for i in (0, 1):
            land_arrival(kind, i)
        slot = y if kind in (ATT, DQ) else xc
        for h in range(groups):
            value = parts[kind, slot, h].astype(F32)
            for i in (0, 1):
                value += landed[kind, i, h].astype(F32)
            results[kind, :, h * HD:(h + 1) * HD] = value.astype(BF16)
        pltpu.make_async_copy(results.at[kind], out, result_sem.at[kind]).start()

    finish(ATT, att_out)
    second_stage(DK, groups - 1)
    finish(DV, dv_out)
    finish(DQ, dq_out)
    finish(DK, dk_out)
    for kind, out in ((ATT, att_out), (DV, dv_out), (DQ, dq_out), (DK, dk_out)):
        pltpu.make_async_copy(results.at[kind], out, result_sem.at[kind]).wait()

    for a in (Q, K, V, G):
        for d in range(1, nz):
            a2a(a, d).wait_send()
        for i in (0, 1, 2):
            slab_total(a, i).wait_send()
    for i in range(3):
        stat_copy(i, y).wait_send()
        delta_copy(i, y).wait_send()
    for kind in range(4):
        for i in (0, 1) if kind in (ATT, DQ) else (0,):
            size = slab // 2 if kind in (ATT, DQ) else slab
            part = parts.at[kind, 0, :, 0:size, :]
            remote(
                part, part, half_send.at[kind, i], half_recv.at[kind, 0, i], y_near[i]
            ).wait_send()
        for i in (0, 1):
            land_total(kind, i).wait_send()


def hand_over(*refs):
    sources, targets, (held, in_sem, out_sem) = refs[:4], refs[4:8], refs[8:]
    loads = [pltpu.make_async_copy(sources[i], held.at[i], in_sem.at[i]) for i in range(4)]
    stores = [pltpu.make_async_copy(held.at[i], targets[i], out_sem.at[i]) for i in range(4)]
    for load in loads:
        load.start()
    for load, store in zip(loads, stores):
        load.wait()
        store.start()
    for store in stores:
        store.wait()


def local(queries, keys, values, out_grad, tile_mask):
    groups = tile_mask.shape[0]
    nz = lax.axis_size("head")
    slab = queries.shape[0] * nz
    units = groups * 4
    out = jax.ShapeDtypeStruct((slab, groups * HD), BF16)
    hbm = pl.BlockSpec(memory_space=pl.ANY)
    dma = pltpu.SemaphoreType.DMA
    results = pl.pallas_call(
        functools.partial(kernel, groups),
        out_shape=(out,) * 4,
        in_specs=[hbm] * 5,
        out_specs=(hbm,) * 4,
        scratch_shapes=[
            pltpu.SMEM(tile_mask.shape, jnp.int32),
            pltpu.VMEM((4, 4, slab, groups * HD), BF16),
            pltpu.VMEM((units, slab, 4 * slab), BF16),
            pltpu.VMEM((groups * 8, 8, 8 * TILE), F32),
            pltpu.VMEM((4, slab, HD), F32),
            pltpu.VMEM((4, 16, 4 * slab), F32),
            pltpu.VMEM((4, 8, 4 * slab), F32),
            pltpu.VMEM((4, slab, HD), F32),
            pltpu.VMEM((4, slab, HD), F32),
            pltpu.VMEM((groups, 4 * slab, HD), BF16),
            pltpu.VMEM((4, 4, groups, slab, HD), BF16),
            pltpu.VMEM((4, groups, slab, HD), BF16),
            pltpu.VMEM((4, 2, groups, slab, HD), BF16),
            pltpu.VMEM((4, slab, groups * HD), BF16),
            dma((4,)),
            dma(()), dma((4, nz)), dma((4, nz)), dma((4,)), dma((4, 3)), dma((4, 3)),
            dma((3,)), dma((3,)), dma((3,)), dma((3,)),
            dma((4, 2)), dma((4, groups, 2)), dma((4, 2)), dma((4, 2)),
        ],
        compiler_params=pltpu.CompilerParams(
            collective_id=0, has_side_effects=True, vmem_limit_bytes=60 << 20
        ),
    )(queries, keys, values, out_grad, tile_mask)
    return pl.pallas_call(
        hand_over,
        out_shape=(out,) * 4,
        in_specs=[hbm] * 4,
        out_specs=(hbm,) * 4,
        scratch_shapes=[pltpu.VMEM((4, slab, groups * HD), BF16), dma((4,)), dma((4,))],
    )(*results)


def solution(mesh):
    return jax.shard_map(
        local,
        mesh=mesh,
        in_specs=(
            P(("dp", "frame", "head"), None),
            P(("dp", "frame", "head"), None),
            P(("dp", "frame", "head"), None),
            P(("dp", "frame", "head"), None),
            P("head", None, None),
        ),
        out_specs=(
            P(("dp", "frame"), "head"),
            P(("dp", "frame"), "head"),
            P(("dp", "frame"), "head"),
            P(("dp", "frame"), "head"),
        ),
        check_vma=False,
    )
```

```python
import functools
import math

import jax
import jax.numpy as jnp
from jax import lax
from jax.experimental import pallas as pl
from jax.experimental.pallas import tpu as pltpu
from jax.sharding import PartitionSpec as P

HD = 128
TILE = 128
NEG = -1e30
S2, S4, S6 = 2, 10, 6
FLOOR = -1e20
LOG2E = 1.4426950408889634
MESH = pl.DeviceIdType.MESH
F32 = jnp.float32
BF16 = jnp.bfloat16

NT = (((1,), (1,)), ((), ()))
NN = (((1,), (0,)), ((), ()))
TN = (((0,), (0,)), ((), ()))

Q, K, V, G = 0, 1, 2, 3


def dot(a, b, dims):
    return lax.dot_general(a, b, dims, preferred_element_type=F32)


def kernel(
    groups,
    q_hbm, k_hbm, v_hbm, g_hbm, mask_hbm,
    att_out, dq_out, dk_out, dv_out,
    mask_ref, allx, probs, bias, rows, stats, deltas, facts, shifts, scaled, parts, halves, landed, results,
    result_sem,
    mask_sem, a2a_send, a2a_recv, own_sem, near_send, near_recv,
    st_send, st_recv, dl_send, dl_recv, half_send, half_recv, land_send, land_recv,
):
    z = lax.axis_index("head")
    nz = lax.axis_size("head")
    f = lax.axis_index("frame")
    y, xc = f // 4, lax.rem(f, 4)
    chunk = q_hbm.shape[0]
    slab = chunk * nz
    width = groups * HD
    scaling = 1.0 / math.sqrt(HD)
    c2 = scaling * LOG2E
    inputs = (q_hbm, k_hbm, v_hbm, g_hbm)

    up, down, far = lax.rem(y + 1, 4), lax.rem(y + 3, 4), lax.rem(y + 2, 4)
    core = lax.rem(xc, 2)
    mate = xc + 1 - 2 * core
    across = lax.rem(xc + 2, 4)
    corner = lax.rem(mate + 2, 4)
    y_near = (up * 4 + xc, down * 4 + xc)
    q_near = (y * 4 + mate, y * 4 + across)

    def own_slot(a):
        return y if a in (Q, G) else xc

    def remote(src, dst, send, recv, frame):
        return pltpu.make_async_remote_copy(
            src_ref=src, dst_ref=dst, send_sem=send, recv_sem=recv,
            device_id={"frame": frame}, device_id_type=MESH,
        )

    mask_copy = pltpu.make_async_copy(mask_hbm, mask_ref, mask_sem)
    mask_copy.start()
    barrier = pltpu.get_barrier_semaphore()
    for d in range(1, nz):
        pl.semaphore_signal(
            barrier, inc=1, device_id={"head": lax.rem(z + d, nz)}, device_id_type=MESH
        )
    for frame in (*y_near, far * 4 + xc, *q_near, y * 4 + corner):
        pl.semaphore_signal(barrier, inc=1, device_id={"frame": frame}, device_id_type=MESH)
    pl.semaphore_wait(barrier, nz - 1 + 6)

    def a2a(a, d):
        to = lax.rem(z + d, nz)
        return pltpu.make_async_remote_copy(
            src_ref=inputs[a].at[:, pl.ds(pl.multiple_of(to * width, width), width)],
            dst_ref=allx.at[a, own_slot(a), pl.ds(pl.multiple_of(z * chunk, chunk), chunk), :],
            send_sem=a2a_send.at[a, d],
            recv_sem=a2a_recv.at[a, d],
            device_id={"head": to},
            device_id_type=MESH,
        )

    def own(a):
        return pltpu.make_async_copy(
            inputs[a].at[:, pl.ds(pl.multiple_of(z * width, width), width)],
            allx.at[a, own_slot(a), pl.ds(pl.multiple_of(z * chunk, chunk), chunk), :],
            own_sem.at[a],
        )

    def distance(step):
        if isinstance(step, int):
            return (step + 1) // 2 if step % 2 else (nz - step // 2) % nz
        return jnp.where(lax.rem(step, 2) == 1, (step + 1) // 2, lax.rem(nz - step // 2, nz))

    for pair in ((K, Q), (V, G)):
        for a in pair:
            own(a).start()
        for step in range(1, nz):
            for a in pair:
                a2a(a, distance(step)).start()

    def span(d, lo=0, size=None):
        start = lax.rem(z + nz - d, nz) * chunk + lo
        size = chunk if size is None else size
        return pl.ds(pl.multiple_of(start, size), size)

    def partner(a, i):
        if a in (Q, G):
            return (up, down, far)[i] * 4 + xc
        return y * 4 + (mate, across, corner)[i]

    def pass_on(a, d, first=False):
        if first:
            own(a).wait()
        else:
            a2a(a, d).wait_recv()
        here = allx.at[a, own_slot(a), span(d), :]
        for i in (2, 0, 1):
            remote(here, here, near_send.at[a, i], near_recv.at[a, i], partner(a, i)).start()

    def slab_total(a, i):
        part = allx.at[a, own_slot(a)]
        return remote(part, part, near_send.at[a, i], near_recv.at[a, i], partner(a, i))

    def arrived(a):
        for i in (0, 1, 2):
            slab_total(a, i).wait_recv()

    def bias_row(row, carry):
        h, qt = row // 8, lax.rem(row, 8)
        qi = (qt // 2) * 8 + xc * 2 + lax.rem(qt, 2)
        for kt in range(8):
            live = mask_ref[h, qi, y * 8 + kt]
            value = jnp.where(live == 1, 0.0, NEG).astype(F32)
            bias[row, :, kt * TILE:(kt + 1) * TILE] = jnp.full((8, TILE), value, F32)
        return carry

    for a in (K, Q, V, G):
        pass_on(a, 0, True)
    mask_copy.wait()
    lax.fori_loop(0, groups * 8, bias_row, 0)
    for step in range(1, nz):
        for a in (K, Q):
            pass_on(a, distance(step))
    lane = lax.broadcasted_iota(jnp.int32, (slab, HD), 1)

    def column(h):
        return pl.ds(pl.multiple_of(h * HD, HD), HD)

    def softmax_step(unit):
        h, s = unit // 4, lax.rem(unit, 4)
        cols = column(h)
        query = allx[Q, s, :, cols]
        key = allx[K, :, :, cols].reshape(4 * slab, HD)
        raw = dot(query, key, NT) * c2
        top = raw[:TILE] + bias[h * 8 + 2 * s, 0:1, :]
        low = raw[TILE:] + bias[h * 8 + 2 * s + 1, 0:1, :]
        for part, block in ((0, top), (1, low)):
            peak = jnp.maximum(jnp.max(block, axis=1, keepdims=True), FLOOR)
            weight = jnp.exp2(block - peak)
            total = jnp.sum(weight, axis=1, keepdims=True)
            probs[unit, part * TILE:(part + 1) * TILE, :] = weight.astype(BF16)
            here = pl.ds(part * TILE, TILE)
            old = rows[s, here, :]
            ln = lane[:TILE]
            rows[s, here, :] = jnp.where(ln == h, peak, jnp.where(ln == 8 + h, total, old))

    rows[...] = jnp.zeros_like(rows)

    def stat_copy(i, slot):
        frame = (up * 4 + xc, far * 4 + xc, down * 4 + xc)[i]
        part = stats.at[slot]
        return remote(part, part, st_send.at[i], st_recv.at[i], frame)

    def share_stats():
        for s in range(4):
            stats[y, :, s * slab:(s + 1) * slab] = rows[s].T[:16]
        for i in range(3):
            stat_copy(i, y).start()

    def one_unit(pair, carry):
        softmax_step(2 * pair)
        softmax_step(2 * pair + 1)
        return carry

    units = groups * 4
    done = 0
    for step in range(1, nz):
        for a in (V, G):
            pass_on(a, distance(step))
        if step == 2:
            for a in (K, Q):
                arrived(a)
        if step % 2 == 0 or step == nz - 1:
            until = units if step == nz - 1 else min(units, done + {2: S2, 4: S4, 6: S6}.get(step, 0))
            lax.fori_loop(done // 2, until // 2, one_unit, 0)
            done = until
    share_stats()

    def delta_copy(i, slot):
        frame = (up * 4 + xc, far * 4 + xc, down * 4 + xc)[i]
        part = deltas.at[slot]
        return remote(part, part, dl_send.at[i], dl_recv.at[i], frame)

    for i in range(3):
        stat_copy(i, (down, far, up)[i]).wait_recv()

    peaks = [stats[d, 0:8, :] for d in range(4)]
    peak = functools.reduce(jnp.maximum, peaks)
    total = sum(stats[d, 8:16, :] * jnp.exp2(peaks[d] - peak) for d in range(4))
    ratio = jnp.exp2(stats[y, 0:8, :] - peak) / total
    blank = jnp.zeros((HD - 8, slab), F32)
    for s in range(4):
        block = jnp.concatenate([ratio[:, s * slab:(s + 1) * slab], blank], axis=0)
        facts[s] = block.T

    def pick(block, index):
        return jnp.sum(jnp.where(lane == index, block, 0.0), axis=1, keepdims=True)

    ATT, DQ, DK, DV = 0, 1, 2, 3

    def half_copies(kind, h):
        half = slab // 2
        if kind in (ATT, DQ):
            return [
                remote(
                    parts.at[kind, far, h, i * half:(i + 1) * half, :],
                    halves.at[kind, h, i * half:(i + 1) * half, :],
                    half_send.at[kind, i], half_recv.at[kind, h, i], y_near[i],
                )
                for i in (0, 1)
            ]
        return [
            remote(
                parts.at[kind, corner, h], halves.at[kind, h],
                half_send.at[kind, 0], half_recv.at[kind, h, 0], q_near[0],
            )
        ]

    def land_copy(kind, h, i):
        slot = (up, down)[i] if kind in (ATT, DQ) else (mate, across)[i]
        frame = y_near[i] if kind in (ATT, DQ) else q_near[i]
        return remote(
            parts.at[kind, slot, h], landed.at[kind, i, h],
            land_send.at[kind, i], land_recv.at[kind, i], frame,
        )

    def first_stage(kind, h):
        for copy in half_copies(kind, h):
            copy.start()
        if kind in (DK, DV):
            land_copy(kind, h, 0).start()

    def second_stage(kind, h):
        half = slab // 2
        for copy in half_copies(kind, h):
            copy.wait_recv()
        if kind in (ATT, DQ):
            for i in (0, 1):
                slot, part = (up, down)[i], slice(i * half, (i + 1) * half)
                mine = parts[kind, slot, h, part, :].astype(F32)
                parts[kind, slot, h, part, :] = (
                    mine + halves[kind, h, part, :].astype(F32)
                ).astype(BF16)
            for i in (0, 1):
                land_copy(kind, h, i).start()
        else:
            mine = parts[kind, across, h].astype(F32)
            parts[kind, across, h] = (mine + halves[kind, h].astype(F32)).astype(BF16)
            land_copy(kind, h, 1).start()

    for a in (V, G):
        arrived(a)

    def attend_head(h, carry):
        cols = column(h)
        value = allx[V, :, :, cols].reshape(4 * slab, HD)
        for s in range(4):
            factor = pick(facts[s], h)
            summed = dot(probs[h * 4 + s], value, NN) * factor
            parts[ATT, s, h] = summed.astype(BF16)
            grad = allx[G, s, :, cols].astype(F32)
            scaled[h, s * slab:(s + 1) * slab, :] = (grad * factor).astype(BF16)
            moved = jnp.sum(grad * summed, axis=1, keepdims=True)
            rows[s] = jnp.where(lane == 16 + h, moved, rows[s])
        first_stage(ATT, h)
        return carry

    lax.fori_loop(0, groups, attend_head, 0)
    for s in range(4):
        deltas[y, :, s * slab:(s + 1) * slab] = rows[s].T[16:24]
    for i in range(3):
        delta_copy(i, y).start()

    def value_head(h, carry):
        turned = scaled[h].T
        weight = probs[pl.ds(h * 4, 4)].reshape(4 * slab, 4 * slab)
        for t in range(4):
            part = dot(turned, weight[:, t * slab:(t + 1) * slab], NN)
            parts[DV, t, h] = part.T.astype(BF16)
        first_stage(DV, h)
        second_stage(ATT, h)
        return carry

    lax.fori_loop(0, groups, value_head, 0)

    for i in range(3):
        delta_copy(i, (down, far, up)[i]).wait_recv()
    delta = sum(deltas[d] for d in range(4)) * ratio
    for s in range(4):
        block = jnp.concatenate([delta[:, s * slab:(s + 1) * slab], blank], axis=0)
        shifts[s] = block.T

    def query_head(h, carry):
        cols = column(h)

        value = allx[V, :, :, cols].reshape(4 * slab, HD)
        key = allx[K, :, :, cols].reshape(4 * slab, HD)
        for s in range(4):
            shift = pick(shifts[s], h)
            moved = dot(scaled[h, s * slab:(s + 1) * slab, :], value, NT)
            score = (probs[h * 4 + s].astype(F32) * (moved - shift)).astype(BF16)
            probs[h * 4 + s] = score
            parts[DQ, s, h] = (dot(score, key, NN) * scaling).astype(BF16)
        first_stage(DQ, h)
        second_stage(DV, h)
        return carry

    lax.fori_loop(0, groups, query_head, 0)

    def key_head(h, carry):
        turned = allx[Q, :, :, column(h)].reshape(4 * slab, HD).T
        score = probs[pl.ds(h * 4, 4)].reshape(4 * slab, 4 * slab)
        for t in range(4):
            part = dot(turned, score[:, t * slab:(t + 1) * slab], NN)
            parts[DK, t, h] = (part.T * scaling).astype(BF16)
        first_stage(DK, h)
        second_stage(DQ, h)

        @pl.when(h > 0)
        def _():
            second_stage(DK, h - 1)

        return carry

    lax.fori_loop(0, groups, key_head, 0)

    def land_total(kind, i):
        frame = y_near[i] if kind in (ATT, DQ) else q_near[i]
        return remote(
            parts.at[kind, 0], landed.at[kind, i], land_send.at[kind, i], land_recv.at[kind, i], frame
        )

    def land_arrival(kind, i):
        back = 1 - i if kind in (ATT, DQ) else i
        land_total(kind, back).wait_recv()

    def finish(kind, out):
        for i in (0, 1):
            land_arrival(kind, i)
        slot = y if kind in (ATT, DQ) else xc
        for h in range(groups):
            value = parts[kind, slot, h].astype(F32)
            for i in (0, 1):
                value += landed[kind, i, h].astype(F32)
            results[kind, :, h * HD:(h + 1) * HD] = value.astype(BF16)
        pltpu.make_async_copy(results.at[kind], out, result_sem.at[kind]).start()

    finish(ATT, att_out)
    second_stage(DK, groups - 1)
    finish(DV, dv_out)
    finish(DQ, dq_out)
    finish(DK, dk_out)
    for kind, out in ((ATT, att_out), (DV, dv_out), (DQ, dq_out), (DK, dk_out)):
        pltpu.make_async_copy(results.at[kind], out, result_sem.at[kind]).wait()

    for a in (Q, K, V, G):
        for d in range(1, nz):
            a2a(a, d).wait_send()
        for i in (0, 1, 2):
            slab_total(a, i).wait_send()
    for i in range(3):
        stat_copy(i, y).wait_send()
        delta_copy(i, y).wait_send()
    for kind in range(4):
        for i in (0, 1) if kind in (ATT, DQ) else (0,):
            size = slab // 2 if kind in (ATT, DQ) else slab
            part = parts.at[kind, 0, :, 0:size, :]
            remote(
                part, part, half_send.at[kind, i], half_recv.at[kind, 0, i], y_near[i]
            ).wait_send()
        for i in (0, 1):
            land_total(kind, i).wait_send()


def hand_over(*refs):
    sources, targets, (held, in_sem, out_sem) = refs[:4], refs[4:8], refs[8:]
    loads = [pltpu.make_async_copy(sources[i], held.at[i], in_sem.at[i]) for i in range(4)]
    stores = [pltpu.make_async_copy(held.at[i], targets[i], out_sem.at[i]) for i in range(4)]
    for load in loads:
        load.start()
    for load, store in zip(loads, stores):
        load.wait()
        store.start()
    for store in stores:
        store.wait()


def local(queries, keys, values, out_grad, tile_mask):
    groups = tile_mask.shape[0]
    nz = lax.axis_size("head")
    slab = queries.shape[0] * nz
    units = groups * 4
    out = jax.ShapeDtypeStruct((slab, groups * HD), BF16)
    hbm = pl.BlockSpec(memory_space=pl.ANY)
    dma = pltpu.SemaphoreType.DMA
    results = pl.pallas_call(
        functools.partial(kernel, groups),
        out_shape=(out,) * 4,
        in_specs=[hbm] * 5,
        out_specs=(hbm,) * 4,
        scratch_shapes=[
            pltpu.SMEM(tile_mask.shape, jnp.int32),
            pltpu.VMEM((4, 4, slab, groups * HD), BF16),
            pltpu.VMEM((units, slab, 4 * slab), BF16),
            pltpu.VMEM((groups * 8, 8, 8 * TILE), F32),
            pltpu.VMEM((4, slab, HD), F32),
            pltpu.VMEM((4, 16, 4 * slab), F32),
            pltpu.VMEM((4, 8, 4 * slab), F32),
            pltpu.VMEM((4, slab, HD), F32),
            pltpu.VMEM((4, slab, HD), F32),
            pltpu.VMEM((groups, 4 * slab, HD), BF16),
            pltpu.VMEM((4, 4, groups, slab, HD), BF16),
            pltpu.VMEM((4, groups, slab, HD), BF16),
            pltpu.VMEM((4, 2, groups, slab, HD), BF16),
            pltpu.VMEM((4, slab, groups * HD), BF16),
            dma((4,)),
            dma(()), dma((4, nz)), dma((4, nz)), dma((4,)), dma((4, 3)), dma((4, 3)),
            dma((3,)), dma((3,)), dma((3,)), dma((3,)),
            dma((4, 2)), dma((4, groups, 2)), dma((4, 2)), dma((4, 2)),
        ],
        compiler_params=pltpu.CompilerParams(
            collective_id=0, has_side_effects=True, vmem_limit_bytes=60 << 20
        ),
    )(queries, keys, values, out_grad, tile_mask)
    return pl.pallas_call(
        hand_over,
        out_shape=(out,) * 4,
        in_specs=[hbm] * 4,
        out_specs=(hbm,) * 4,
        scratch_shapes=[pltpu.VMEM((4, slab, groups * HD), BF16), dma((4,)), dma((4,))],
    )(*results)


def solution(mesh):
    return jax.shard_map(
        local,
        mesh=mesh,
        in_specs=(
            P(("dp", "frame", "head"), None),
            P(("dp", "frame", "head"), None),
            P(("dp", "frame", "head"), None),
            P(("dp", "frame", "head"), None),
            P("head", None, None),
        ),
        out_specs=(
            P(("dp", "frame"), "head"),
            P(("dp", "frame"), "head"),
            P(("dp", "frame"), "head"),
            P(("dp", "frame"), "head"),
        ),
        check_vma=False,
    )
```

```python
import functools
import math

import jax
import jax.numpy as jnp
from jax import lax
from jax.experimental import pallas as pl
from jax.experimental.pallas import tpu as pltpu
from jax.sharding import PartitionSpec as P

HD = 128
TILE = 128
NEG = -1e30
S2, S4, S6 = 0, 10, 6
FLOOR = -1e20
LOG2E = 1.4426950408889634
MESH = pl.DeviceIdType.MESH
F32 = jnp.float32
BF16 = jnp.bfloat16

NT = (((1,), (1,)), ((), ()))
NN = (((1,), (0,)), ((), ()))
TN = (((0,), (0,)), ((), ()))

Q, K, V, G = 0, 1, 2, 3


def dot(a, b, dims):
    return lax.dot_general(a, b, dims, preferred_element_type=F32)


def kernel(
    groups,
    q_hbm, k_hbm, v_hbm, g_hbm, mask_hbm,
    att_out, dq_out, dk_out, dv_out,
    mask_ref, allx, probs, bias, rows, stats, deltas, facts, shifts, scaled, parts, halves, landed, results,
    result_sem,
    mask_sem, a2a_send, a2a_recv, own_sem, near_send, near_recv,
    st_send, st_recv, dl_send, dl_recv, half_send, half_recv, land_send, land_recv,
):
    z = lax.axis_index("head")
    nz = lax.axis_size("head")
    f = lax.axis_index("frame")
    y, xc = f // 4, lax.rem(f, 4)
    chunk = q_hbm.shape[0]
    slab = chunk * nz
    width = groups * HD
    scaling = 1.0 / math.sqrt(HD)
    c2 = scaling * LOG2E
    inputs = (q_hbm, k_hbm, v_hbm, g_hbm)

    up, down, far = lax.rem(y + 1, 4), lax.rem(y + 3, 4), lax.rem(y + 2, 4)
    core = lax.rem(xc, 2)
    mate = xc + 1 - 2 * core
    across = lax.rem(xc + 2, 4)
    corner = lax.rem(mate + 2, 4)
    y_near = (up * 4 + xc, down * 4 + xc)
    q_near = (y * 4 + mate, y * 4 + across)

    def own_slot(a):
        return y if a in (Q, G) else xc

    def remote(src, dst, send, recv, frame):
        return pltpu.make_async_remote_copy(
            src_ref=src, dst_ref=dst, send_sem=send, recv_sem=recv,
            device_id={"frame": frame}, device_id_type=MESH,
        )

    mask_copy = pltpu.make_async_copy(mask_hbm, mask_ref, mask_sem)
    mask_copy.start()
    barrier = pltpu.get_barrier_semaphore()
    for d in range(1, nz):
        pl.semaphore_signal(
            barrier, inc=1, device_id={"head": lax.rem(z + d, nz)}, device_id_type=MESH
        )
    for frame in (*y_near, far * 4 + xc, *q_near, y * 4 + corner):
        pl.semaphore_signal(barrier, inc=1, device_id={"frame": frame}, device_id_type=MESH)
    pl.semaphore_wait(barrier, nz - 1 + 6)

    def a2a(a, d):
        to = lax.rem(z + d, nz)
        return pltpu.make_async_remote_copy(
            src_ref=inputs[a].at[:, pl.ds(pl.multiple_of(to * width, width), width)],
            dst_ref=allx.at[a, own_slot(a), pl.ds(pl.multiple_of(z * chunk, chunk), chunk), :],
            send_sem=a2a_send.at[a, d],
            recv_sem=a2a_recv.at[a, d],
            device_id={"head": to},
            device_id_type=MESH,
        )

    def own(a):
        return pltpu.make_async_copy(
            inputs[a].at[:, pl.ds(pl.multiple_of(z * width, width), width)],
            allx.at[a, own_slot(a), pl.ds(pl.multiple_of(z * chunk, chunk), chunk), :],
            own_sem.at[a],
        )

    def distance(step):
        if isinstance(step, int):
            return (step + 1) // 2 if step % 2 else (nz - step // 2) % nz
        return jnp.where(lax.rem(step, 2) == 1, (step + 1) // 2, lax.rem(nz - step // 2, nz))

    for pair in ((K, Q), (V, G)):
        for a in pair:
            own(a).start()
        for step in range(1, nz):
            for a in pair:
                a2a(a, distance(step)).start()

    def span(d, lo=0, size=None):
        start = lax.rem(z + nz - d, nz) * chunk + lo
        size = chunk if size is None else size
        return pl.ds(pl.multiple_of(start, size), size)

    def partner(a, i):
        if a in (Q, G):
            return (up, down, far)[i] * 4 + xc
        return y * 4 + (mate, across, corner)[i]

    def pass_on(a, d, first=False):
        if first:
            own(a).wait()
        else:
            a2a(a, d).wait_recv()
        here = allx.at[a, own_slot(a), span(d), :]
        for i in (2, 0, 1):
            remote(here, here, near_send.at[a, i], near_recv.at[a, i], partner(a, i)).start()

    def slab_total(a, i):
        part = allx.at[a, own_slot(a)]
        return remote(part, part, near_send.at[a, i], near_recv.at[a, i], partner(a, i))

    def arrived(a):
        for i in (0, 1, 2):
            slab_total(a, i).wait_recv()

    def bias_row(row, carry):
        h, qt = row // 8, lax.rem(row, 8)
        qi = (qt // 2) * 8 + xc * 2 + lax.rem(qt, 2)
        for kt in range(8):
            live = mask_ref[h, qi, y * 8 + kt]
            value = jnp.where(live == 1, 0.0, NEG).astype(F32)
            bias[row, :, kt * TILE:(kt + 1) * TILE] = jnp.full((8, TILE), value, F32)
        return carry

    for a in (K, Q, V, G):
        pass_on(a, 0, True)
    mask_copy.wait()
    lax.fori_loop(0, groups * 8, bias_row, 0)
    for step in range(1, nz):
        for a in (K, Q):
            pass_on(a, distance(step))
    lane = lax.broadcasted_iota(jnp.int32, (slab, HD), 1)

    def column(h):
        return pl.ds(pl.multiple_of(h * HD, HD), HD)

    def softmax_step(unit):
        h, s = unit // 4, lax.rem(unit, 4)
        cols = column(h)
        query = allx[Q, s, :, cols]
        key = allx[K, :, :, cols].reshape(4 * slab, HD)
        raw = dot(query, key, NT) * c2
        top = raw[:TILE] + bias[h * 8 + 2 * s, 0:1, :]
        low = raw[TILE:] + bias[h * 8 + 2 * s + 1, 0:1, :]
        for part, block in ((0, top), (1, low)):
            peak = jnp.maximum(jnp.max(block, axis=1, keepdims=True), FLOOR)
            weight = jnp.exp2(block - peak)
            total = jnp.sum(weight, axis=1, keepdims=True)
            probs[unit, part * TILE:(part + 1) * TILE, :] = weight.astype(BF16)
            here = pl.ds(part * TILE, TILE)
            old = rows[s, here, :]
            ln = lane[:TILE]
            rows[s, here, :] = jnp.where(ln == h, peak, jnp.where(ln == 8 + h, total, old))

    rows[...] = jnp.zeros_like(rows)

    def stat_copy(i, slot):
        frame = (up * 4 + xc, far * 4 + xc, down * 4 + xc)[i]
        part = stats.at[slot]
        return remote(part, part, st_send.at[i], st_recv.at[i], frame)

    def share_stats():
        for s in range(4):
            stats[y, :, s * slab:(s + 1) * slab] = rows[s].T[:16]
        for i in range(3):
            stat_copy(i, y).start()

    def one_unit(pair, carry):
        softmax_step(2 * pair)
        softmax_step(2 * pair + 1)
        return carry

    units = groups * 4
    done = 0
    for step in range(1, nz):
        for a in (V, G):
            pass_on(a, distance(step))
        if step == 2:
            for a in (K, Q):
                arrived(a)
        if step % 2 == 0 or step == nz - 1:
            until = units if step == nz - 1 else min(units, done + {2: S2, 4: S4, 6: S6}.get(step, 0))
            lax.fori_loop(done // 2, until // 2, one_unit, 0)
            done = until
    share_stats()

    def delta_copy(i, slot):
        frame = (up * 4 + xc, far * 4 + xc, down * 4 + xc)[i]
        part = deltas.at[slot]
        return remote(part, part, dl_send.at[i], dl_recv.at[i], frame)

    for i in range(3):
        stat_copy(i, (down, far, up)[i]).wait_recv()

    peaks = [stats[d, 0:8, :] for d in range(4)]
    peak = functools.reduce(jnp.maximum, peaks)
    total = sum(stats[d, 8:16, :] * jnp.exp2(peaks[d] - peak) for d in range(4))
    ratio = jnp.exp2(stats[y, 0:8, :] - peak) / total
    blank = jnp.zeros((HD - 8, slab), F32)
    for s in range(4):
        block = jnp.concatenate([ratio[:, s * slab:(s + 1) * slab], blank], axis=0)
        facts[s] = block.T

    def pick(block, index):
        return jnp.sum(jnp.where(lane == index, block, 0.0), axis=1, keepdims=True)

    ATT, DQ, DK, DV = 0, 1, 2, 3

    def half_copies(kind, h):
        half = slab // 2
        if kind in (ATT, DQ):
            return [
                remote(
                    parts.at[kind, far, h, i * half:(i + 1) * half, :],
                    halves.at[kind, h, i * half:(i + 1) * half, :],
                    half_send.at[kind, i], half_recv.at[kind, h, i], y_near[i],
                )
                for i in (0, 1)
            ]
        return [
            remote(
                parts.at[kind, corner, h], halves.at[kind, h],
                half_send.at[kind, 0], half_recv.at[kind, h, 0], q_near[0],
            )
        ]

    def land_copy(kind, h, i):
        slot = (up, down)[i] if kind in (ATT, DQ) else (mate, across)[i]
        frame = y_near[i] if kind in (ATT, DQ) else q_near[i]
        return remote(
            parts.at[kind, slot, h], landed.at[kind, i, h],
            land_send.at[kind, i], land_recv.at[kind, i], frame,
        )

    def first_stage(kind, h):
        for copy in half_copies(kind, h):
            copy.start()
        if kind in (DK, DV):
            land_copy(kind, h, 0).start()

    def second_stage(kind, h):
        half = slab // 2
        for copy in half_copies(kind, h):
            copy.wait_recv()
        if kind in (ATT, DQ):
            for i in (0, 1):
                slot, part = (up, down)[i], slice(i * half, (i + 1) * half)
                mine = parts[kind, slot, h, part, :].astype(F32)
                parts[kind, slot, h, part, :] = (
                    mine + halves[kind, h, part, :].astype(F32)
                ).astype(BF16)
            for i in (0, 1):
                land_copy(kind, h, i).start()
        else:
            mine = parts[kind, across, h].astype(F32)
            parts[kind, across, h] = (mine + halves[kind, h].astype(F32)).astype(BF16)
            land_copy(kind, h, 1).start()

    for a in (V, G):
        arrived(a)

    def attend_head(h, carry):
        cols = column(h)
        value = allx[V, :, :, cols].reshape(4 * slab, HD)
        for s in range(4):
            factor = pick(facts[s], h)
            summed = dot(probs[h * 4 + s], value, NN) * factor
            parts[ATT, s, h] = summed.astype(BF16)
            grad = allx[G, s, :, cols].astype(F32)
            scaled[h, s * slab:(s + 1) * slab, :] = (grad * factor).astype(BF16)
            moved = jnp.sum(grad * summed, axis=1, keepdims=True)
            rows[s] = jnp.where(lane == 16 + h, moved, rows[s])
        first_stage(ATT, h)
        return carry

    lax.fori_loop(0, groups, attend_head, 0)
    for s in range(4):
        deltas[y, :, s * slab:(s + 1) * slab] = rows[s].T[16:24]
    for i in range(3):
        delta_copy(i, y).start()

    def value_head(h, carry):
        turned = scaled[h].T
        weight = probs[pl.ds(h * 4, 4)].reshape(4 * slab, 4 * slab)
        for t in range(4):
            part = dot(turned, weight[:, t * slab:(t + 1) * slab], NN)
            parts[DV, t, h] = part.T.astype(BF16)
        first_stage(DV, h)
        second_stage(ATT, h)
        return carry

    lax.fori_loop(0, groups, value_head, 0)

    for i in range(3):
        delta_copy(i, (down, far, up)[i]).wait_recv()
    delta = sum(deltas[d] for d in range(4)) * ratio
    for s in range(4):
        block = jnp.concatenate([delta[:, s * slab:(s + 1) * slab], blank], axis=0)
        shifts[s] = block.T

    def query_head(h, carry):
        cols = column(h)

        value = allx[V, :, :, cols].reshape(4 * slab, HD)
        key = allx[K, :, :, cols].reshape(4 * slab, HD)
        for s in range(4):
            shift = pick(shifts[s], h)
            moved = dot(scaled[h, s * slab:(s + 1) * slab, :], value, NT)
            score = (probs[h * 4 + s].astype(F32) * (moved - shift)).astype(BF16)
            probs[h * 4 + s] = score
            parts[DQ, s, h] = (dot(score, key, NN) * scaling).astype(BF16)
        first_stage(DQ, h)
        second_stage(DV, h)
        return carry

    lax.fori_loop(0, groups, query_head, 0)

    def key_head(h, carry):
        turned = allx[Q, :, :, column(h)].reshape(4 * slab, HD).T
        score = probs[pl.ds(h * 4, 4)].reshape(4 * slab, 4 * slab)
        for t in range(4):
            part = dot(turned, score[:, t * slab:(t + 1) * slab], NN)
            parts[DK, t, h] = (part.T * scaling).astype(BF16)
        first_stage(DK, h)
        second_stage(DQ, h)

        @pl.when(h > 0)
        def _():
            second_stage(DK, h - 1)

        return carry

    lax.fori_loop(0, groups, key_head, 0)

    def land_total(kind, i):
        frame = y_near[i] if kind in (ATT, DQ) else q_near[i]
        return remote(
            parts.at[kind, 0], landed.at[kind, i], land_send.at[kind, i], land_recv.at[kind, i], frame
        )

    def land_arrival(kind, i):
        back = 1 - i if kind in (ATT, DQ) else i
        land_total(kind, back).wait_recv()

    def finish(kind, out):
        for i in (0, 1):
            land_arrival(kind, i)
        slot = y if kind in (ATT, DQ) else xc
        for h in range(groups):
            value = parts[kind, slot, h].astype(F32)
            for i in (0, 1):
                value += landed[kind, i, h].astype(F32)
            results[kind, :, h * HD:(h + 1) * HD] = value.astype(BF16)
        pltpu.make_async_copy(results.at[kind], out, result_sem.at[kind]).start()

    finish(ATT, att_out)
    second_stage(DK, groups - 1)
    finish(DV, dv_out)
    finish(DQ, dq_out)
    finish(DK, dk_out)
    for kind, out in ((ATT, att_out), (DV, dv_out), (DQ, dq_out), (DK, dk_out)):
        pltpu.make_async_copy(results.at[kind], out, result_sem.at[kind]).wait()

    for a in (Q, K, V, G):
        for d in range(1, nz):
            a2a(a, d).wait_send()
        for i in (0, 1, 2):
            slab_total(a, i).wait_send()
    for i in range(3):
        stat_copy(i, y).wait_send()
        delta_copy(i, y).wait_send()
    for kind in range(4):
        for i in (0, 1) if kind in (ATT, DQ) else (0,):
            size = slab // 2 if kind in (ATT, DQ) else slab
            part = parts.at[kind, 0, :, 0:size, :]
            remote(
                part, part, half_send.at[kind, i], half_recv.at[kind, 0, i], y_near[i]
            ).wait_send()
        for i in (0, 1):
            land_total(kind, i).wait_send()


def hand_over(*refs):
    sources, targets, (held, in_sem, out_sem) = refs[:4], refs[4:8], refs[8:]
    loads = [pltpu.make_async_copy(sources[i], held.at[i], in_sem.at[i]) for i in range(4)]
    stores = [pltpu.make_async_copy(held.at[i], targets[i], out_sem.at[i]) for i in range(4)]
    for load in loads:
        load.start()
    for load, store in zip(loads, stores):
        load.wait()
        store.start()
    for store in stores:
        store.wait()


def local(queries, keys, values, out_grad, tile_mask):
    groups = tile_mask.shape[0]
    nz = lax.axis_size("head")
    slab = queries.shape[0] * nz
    units = groups * 4
    out = jax.ShapeDtypeStruct((slab, groups * HD), BF16)
    hbm = pl.BlockSpec(memory_space=pl.ANY)
    dma = pltpu.SemaphoreType.DMA
    results = pl.pallas_call(
        functools.partial(kernel, groups),
        out_shape=(out,) * 4,
        in_specs=[hbm] * 5,
        out_specs=(hbm,) * 4,
        scratch_shapes=[
            pltpu.SMEM(tile_mask.shape, jnp.int32),
            pltpu.VMEM((4, 4, slab, groups * HD), BF16),
            pltpu.VMEM((units, slab, 4 * slab), BF16),
            pltpu.VMEM((groups * 8, 8, 8 * TILE), F32),
            pltpu.VMEM((4, slab, HD), F32),
            pltpu.VMEM((4, 16, 4 * slab), F32),
            pltpu.VMEM((4, 8, 4 * slab), F32),
            pltpu.VMEM((4, slab, HD), F32),
            pltpu.VMEM((4, slab, HD), F32),
            pltpu.VMEM((groups, 4 * slab, HD), BF16),
            pltpu.VMEM((4, 4, groups, slab, HD), BF16),
            pltpu.VMEM((4, groups, slab, HD), BF16),
            pltpu.VMEM((4, 2, groups, slab, HD), BF16),
            pltpu.VMEM((4, slab, groups * HD), BF16),
            dma((4,)),
            dma(()), dma((4, nz)), dma((4, nz)), dma((4,)), dma((4, 3)), dma((4, 3)),
            dma((3,)), dma((3,)), dma((3,)), dma((3,)),
            dma((4, 2)), dma((4, groups, 2)), dma((4, 2)), dma((4, 2)),
        ],
        compiler_params=pltpu.CompilerParams(
            collective_id=0, has_side_effects=True, vmem_limit_bytes=60 << 20
        ),
    )(queries, keys, values, out_grad, tile_mask)
    return pl.pallas_call(
        hand_over,
        out_shape=(out,) * 4,
        in_specs=[hbm] * 4,
        out_specs=(hbm,) * 4,
        scratch_shapes=[pltpu.VMEM((4, slab, groups * HD), BF16), dma((4,)), dma((4,))],
    )(*results)


def solution(mesh):
    return jax.shard_map(
        local,
        mesh=mesh,
        in_specs=(
            P(("dp", "frame", "head"), None),
            P(("dp", "frame", "head"), None),
            P(("dp", "frame", "head"), None),
            P(("dp", "frame", "head"), None),
            P("head", None, None),
        ),
        out_specs=(
            P(("dp", "frame"), "head"),
            P(("dp", "frame"), "head"),
            P(("dp", "frame"), "head"),
            P(("dp", "frame"), "head"),
        ),
        check_vma=False,
    )
```

```python
import functools
import math

import jax
import jax.numpy as jnp
from jax import lax
from jax.experimental import pallas as pl
from jax.experimental.pallas import tpu as pltpu
from jax.sharding import PartitionSpec as P

HD = 128
TILE = 128
NEG = -1e30
S2, S4, S6 = 2, 10, 6
FLOOR = -1e20
LOG2E = 1.4426950408889634
MESH = pl.DeviceIdType.MESH
F32 = jnp.float32
BF16 = jnp.bfloat16

NT = (((1,), (1,)), ((), ()))
NN = (((1,), (0,)), ((), ()))
TN = (((0,), (0,)), ((), ()))

Q, K, V, G = 0, 1, 2, 3


def dot(a, b, dims):
    return lax.dot_general(a, b, dims, preferred_element_type=F32)


def kernel(
    groups,
    q_hbm, k_hbm, v_hbm, g_hbm, mask_hbm,
    att_out, dq_out, dk_out, dv_out,
    mask_ref, allx, probs, bias, rows, stats, deltas, facts, shifts, scaled, parts, halves, landed, results,
    result_sem,
    mask_sem, a2a_send, a2a_recv, own_sem, near_send, near_recv,
    st_send, st_recv, dl_send, dl_recv, half_send, half_recv, land_send, land_recv,
):
    z = lax.axis_index("head")
    nz = lax.axis_size("head")
    f = lax.axis_index("frame")
    y, xc = f // 4, lax.rem(f, 4)
    chunk = q_hbm.shape[0]
    slab = chunk * nz
    width = groups * HD
    scaling = 1.0 / math.sqrt(HD)
    c2 = scaling * LOG2E
    inputs = (q_hbm, k_hbm, v_hbm, g_hbm)

    up, down, far = lax.rem(y + 1, 4), lax.rem(y + 3, 4), lax.rem(y + 2, 4)
    core = lax.rem(xc, 2)
    mate = xc + 1 - 2 * core
    across = lax.rem(xc + 2, 4)
    corner = lax.rem(mate + 2, 4)
    y_near = (up * 4 + xc, down * 4 + xc)
    q_near = (y * 4 + mate, y * 4 + across)

    def own_slot(a):
        return y if a in (Q, G) else xc

    def remote(src, dst, send, recv, frame):
        return pltpu.make_async_remote_copy(
            src_ref=src, dst_ref=dst, send_sem=send, recv_sem=recv,
            device_id={"frame": frame}, device_id_type=MESH,
        )

    mask_copy = pltpu.make_async_copy(mask_hbm, mask_ref, mask_sem)
    mask_copy.start()
    barrier = pltpu.get_barrier_semaphore()
    for d in range(1, nz):
        pl.semaphore_signal(
            barrier, inc=1, device_id={"head": lax.rem(z + d, nz)}, device_id_type=MESH
        )
    for frame in (*y_near, far * 4 + xc, *q_near, y * 4 + corner):
        pl.semaphore_signal(barrier, inc=1, device_id={"frame": frame}, device_id_type=MESH)
    pl.semaphore_wait(barrier, nz - 1 + 6)

    def a2a(a, d):
        to = lax.rem(z + d, nz)
        return pltpu.make_async_remote_copy(
            src_ref=inputs[a].at[:, pl.ds(pl.multiple_of(to * width, width), width)],
            dst_ref=allx.at[a, own_slot(a), pl.ds(pl.multiple_of(z * chunk, chunk), chunk), :],
            send_sem=a2a_send.at[a, d],
            recv_sem=a2a_recv.at[a, d],
            device_id={"head": to},
            device_id_type=MESH,
        )

    def own(a):
        return pltpu.make_async_copy(
            inputs[a].at[:, pl.ds(pl.multiple_of(z * width, width), width)],
            allx.at[a, own_slot(a), pl.ds(pl.multiple_of(z * chunk, chunk), chunk), :],
            own_sem.at[a],
        )

    def distance(step):
        if isinstance(step, int):
            return (step + 1) // 2 if step % 2 else (nz - step // 2) % nz
        return jnp.where(lax.rem(step, 2) == 1, (step + 1) // 2, lax.rem(nz - step // 2, nz))

    for pair in ((K, Q), (V, G)):
        for a in pair:
            own(a).start()
        for step in range(1, nz):
            for a in pair:
                a2a(a, distance(step)).start()

    def span(d, lo=0, size=None):
        start = lax.rem(z + nz - d, nz) * chunk + lo
        size = chunk if size is None else size
        return pl.ds(pl.multiple_of(start, size), size)

    def partner(a, i):
        if a in (Q, G):
            return (up, down, far)[i] * 4 + xc
        return y * 4 + (mate, across, corner)[i]

    def pass_on(a, d, first=False):
        if first:
            own(a).wait()
        else:
            a2a(a, d).wait_recv()
        here = allx.at[a, own_slot(a), span(d), :]
        for i in (2, 0, 1):
            remote(here, here, near_send.at[a, i], near_recv.at[a, i], partner(a, i)).start()

    def slab_total(a, i):
        part = allx.at[a, own_slot(a)]
        return remote(part, part, near_send.at[a, i], near_recv.at[a, i], partner(a, i))

    def arrived(a):
        for i in (0, 1, 2):
            slab_total(a, i).wait_recv()

    def bias_row(row, carry):
        h, qt = row // 8, lax.rem(row, 8)
        qi = (qt // 2) * 8 + xc * 2 + lax.rem(qt, 2)
        for kt in range(8):
            live = mask_ref[h, qi, y * 8 + kt]
            value = jnp.where(live == 1, 0.0, NEG).astype(F32)
            bias[row, :, kt * TILE:(kt + 1) * TILE] = jnp.full((8, TILE), value, F32)
        return carry

    for a in (K, Q, V, G):
        pass_on(a, 0, True)
    mask_copy.wait()
    lax.fori_loop(0, groups * 8, bias_row, 0)
    for step in range(1, nz):
        for a in (K, Q):
            pass_on(a, distance(step))
    lane = lax.broadcasted_iota(jnp.int32, (slab, HD), 1)

    def column(h):
        return pl.ds(pl.multiple_of(h * HD, HD), HD)

    def softmax_step(unit):
        h, s = unit // 4, lax.rem(unit, 4)
        cols = column(h)
        query = allx[Q, s, :, cols]
        key = allx[K, :, :, cols].reshape(4 * slab, HD)
        raw = dot(query, key, NT) * c2
        top = raw[:TILE] + bias[h * 8 + 2 * s, 0:1, :]
        low = raw[TILE:] + bias[h * 8 + 2 * s + 1, 0:1, :]
        for part, block in ((0, top), (1, low)):
            peak = jnp.maximum(jnp.max(block, axis=1, keepdims=True), FLOOR)
            weight = jnp.exp2(block - peak)
            total = jnp.sum(weight, axis=1, keepdims=True)
            probs[unit, part * TILE:(part + 1) * TILE, :] = weight.astype(BF16)
            here = pl.ds(part * TILE, TILE)
            old = rows[s, here, :]
            ln = lane[:TILE]
            rows[s, here, :] = jnp.where(ln == h, peak, jnp.where(ln == 8 + h, total, old))

    rows[...] = jnp.zeros_like(rows)

    def stat_copy(i, slot):
        frame = (up * 4 + xc, far * 4 + xc, down * 4 + xc)[i]
        part = stats.at[slot]
        return remote(part, part, st_send.at[i], st_recv.at[i], frame)

    def share_stats():
        for s in range(4):
            stats[y, :, s * slab:(s + 1) * slab] = rows[s].T[:16]
        for i in range(3):
            stat_copy(i, y).start()

    def one_unit(pair, carry):
        softmax_step(2 * pair)
        softmax_step(2 * pair + 1)
        return carry

    units = groups * 4
    done = 0
    for step in range(1, nz):
        for a in (V, G):
            pass_on(a, distance(step))
        if step == 2:
            for a in (K, Q):
                arrived(a)
        if step % 2 == 0 or step == nz - 1:
            until = units if step == nz - 1 else min(units, done + {2: S2, 4: S4, 6: S6}.get(step, 0))
            lax.fori_loop(done // 2, until // 2, one_unit, 0)
            done = until
    share_stats()

    def delta_copy(i, slot):
        frame = (up * 4 + xc, far * 4 + xc, down * 4 + xc)[i]
        part = deltas.at[slot]
        return remote(part, part, dl_send.at[i], dl_recv.at[i], frame)

    for i in range(3):
        stat_copy(i, (down, far, up)[i]).wait_recv()

    peaks = [stats[d, 0:8, :] for d in range(4)]
    peak = functools.reduce(jnp.maximum, peaks)
    total = sum(stats[d, 8:16, :] * jnp.exp2(peaks[d] - peak) for d in range(4))
    ratio = jnp.exp2(stats[y, 0:8, :] - peak) / total
    blank = jnp.zeros((HD - 8, slab), F32)
    for s in range(4):
        block = jnp.concatenate([ratio[:, s * slab:(s + 1) * slab], blank], axis=0)
        facts[s] = block.T

    def pick(block, index):
        return jnp.sum(jnp.where(lane == index, block, 0.0), axis=1, keepdims=True)

    ATT, DQ, DK, DV = 0, 1, 2, 3

    def half_copies(kind, h):
        half = slab // 2
        if kind in (ATT, DQ):
            return [
                remote(
                    parts.at[kind, far, h, i * half:(i + 1) * half, :],
                    halves.at[kind, h, i * half:(i + 1) * half, :],
                    half_send.at[kind, i], half_recv.at[kind, h, i], y_near[i],
                )
                for i in (0, 1)
            ]
        return [
            remote(
                parts.at[kind, corner, h], halves.at[kind, h],
                half_send.at[kind, 0], half_recv.at[kind, h, 0], q_near[0],
            )
        ]

    def land_copy(kind, h, i):
        slot = (up, down)[i] if kind in (ATT, DQ) else (mate, across)[i]
        frame = y_near[i] if kind in (ATT, DQ) else q_near[i]
        return remote(
            parts.at[kind, slot, h], landed.at[kind, i, h],
            land_send.at[kind, i], land_recv.at[kind, i], frame,
        )

    def first_stage(kind, h):
        for copy in half_copies(kind, h):
            copy.start()
        if kind in (DK, DV):
            land_copy(kind, h, 0).start()

    def second_stage(kind, h):
        half = slab // 2
        for copy in half_copies(kind, h):
            copy.wait_recv()
        if kind in (ATT, DQ):
            for i in (0, 1):
                slot, part = (up, down)[i], slice(i * half, (i + 1) * half)
                mine = parts[kind, slot, h, part, :].astype(F32)
                parts[kind, slot, h, part, :] = (
                    mine + halves[kind, h, part, :].astype(F32)
                ).astype(BF16)
            for i in (0, 1):
                land_copy(kind, h, i).start()
        else:
            mine = parts[kind, across, h].astype(F32)
            parts[kind, across, h] = (mine + halves[kind, h].astype(F32)).astype(BF16)
            land_copy(kind, h, 1).start()

    for a in (V, G):
        arrived(a)

    def attend_head(h, carry):
        cols = column(h)
        value = allx[V, :, :, cols].reshape(4 * slab, HD)
        for s in range(4):
            factor = pick(facts[s], h)
            summed = dot(probs[h * 4 + s], value, NN) * factor
            parts[ATT, s, h] = summed.astype(BF16)
            grad = allx[G, s, :, cols].astype(F32)
            scaled[h, s * slab:(s + 1) * slab, :] = (grad * factor).astype(BF16)
            moved = jnp.sum(grad * summed, axis=1, keepdims=True)
            rows[s] = jnp.where(lane == 16 + h, moved, rows[s])
        first_stage(ATT, h)
        return carry

    lax.fori_loop(0, groups, attend_head, 0)
    for s in range(4):
        deltas[y, :, s * slab:(s + 1) * slab] = rows[s].T[16:24]
    for i in range(3):
        delta_copy(i, y).start()

    def value_head(h, carry):
        turned = scaled[h].T
        weight = probs[pl.ds(h * 4, 4)].reshape(4 * slab, 4 * slab)
        for t in range(4):
            part = dot(turned, weight[:, t * slab:(t + 1) * slab], NN)
            parts[DV, t, h] = part.T.astype(BF16)
        first_stage(DV, h)
        second_stage(ATT, h)
        return carry

    lax.fori_loop(0, groups, value_head, 0)

    for i in range(3):
        delta_copy(i, (down, far, up)[i]).wait_recv()
    delta = sum(deltas[d] for d in range(4)) * ratio
    for s in range(4):
        block = jnp.concatenate([delta[:, s * slab:(s + 1) * slab], blank], axis=0)
        shifts[s] = block.T

    def query_head(h, carry):
        cols = column(h)

        value = allx[V, :, :, cols].reshape(4 * slab, HD)
        key = allx[K, :, :, cols].reshape(4 * slab, HD)
        for s in range(4):
            shift = pick(shifts[s], h)
            moved = dot(scaled[h, s * slab:(s + 1) * slab, :], value, NT)
            score = (probs[h * 4 + s].astype(F32) * (moved - shift)).astype(BF16)
            probs[h * 4 + s] = score
            parts[DQ, s, h] = (dot(score, key, NN) * scaling).astype(BF16)
        first_stage(DQ, h)
        second_stage(DV, h)
        return carry

    lax.fori_loop(0, groups, query_head, 0)

    def key_head(h, carry):
        turned = allx[Q, :, :, column(h)].reshape(4 * slab, HD).T
        score = probs[pl.ds(h * 4, 4)].reshape(4 * slab, 4 * slab)
        for t in range(4):
            part = dot(turned, score[:, t * slab:(t + 1) * slab], NN)
            parts[DK, t, h] = (part.T * scaling).astype(BF16)
        first_stage(DK, h)
        second_stage(DQ, h)

        @pl.when(h > 0)
        def _():
            second_stage(DK, h - 1)

        return carry

    lax.fori_loop(0, groups, key_head, 0)

    def land_total(kind, i):
        frame = y_near[i] if kind in (ATT, DQ) else q_near[i]
        return remote(
            parts.at[kind, 0], landed.at[kind, i], land_send.at[kind, i], land_recv.at[kind, i], frame
        )

    def land_arrival(kind, i):
        back = 1 - i if kind in (ATT, DQ) else i
        land_total(kind, back).wait_recv()

    def finish(kind, out):
        for i in (0, 1):
            land_arrival(kind, i)
        slot = y if kind in (ATT, DQ) else xc
        for h in range(groups):
            value = parts[kind, slot, h].astype(F32)
            for i in (0, 1):
                value += landed[kind, i, h].astype(F32)
            results[kind, :, h * HD:(h + 1) * HD] = value.astype(BF16)
        pltpu.make_async_copy(results.at[kind], out, result_sem.at[kind]).start()

    finish(ATT, att_out)
    second_stage(DK, groups - 1)
    finish(DV, dv_out)
    finish(DQ, dq_out)
    finish(DK, dk_out)
    for kind, out in ((ATT, att_out), (DV, dv_out), (DQ, dq_out), (DK, dk_out)):
        pltpu.make_async_copy(results.at[kind], out, result_sem.at[kind]).wait()

    for a in (Q, K, V, G):
        for d in range(1, nz):
            a2a(a, d).wait_send()
        for i in (0, 1, 2):
            slab_total(a, i).wait_send()
    for i in range(3):
        stat_copy(i, y).wait_send()
        delta_copy(i, y).wait_send()
    for kind in range(4):
        for i in (0, 1) if kind in (ATT, DQ) else (0,):
            size = slab // 2 if kind in (ATT, DQ) else slab
            part = parts.at[kind, 0, :, 0:size, :]
            remote(
                part, part, half_send.at[kind, i], half_recv.at[kind, 0, i], y_near[i]
            ).wait_send()
        for i in (0, 1):
            land_total(kind, i).wait_send()


def hand_over(*refs):
    sources, targets, (held, in_sem, out_sem) = refs[:4], refs[4:8], refs[8:]
    half = held.shape[1] // 2
    cuts = [(i, j, pl.ds(j * half, half)) for i in range(4) for j in (0, 1)]
    loads = [
        pltpu.make_async_copy(sources[i].at[c], held.at[i, c], in_sem.at[i, j]) for i, j, c in cuts
    ]
    stores = [
        pltpu.make_async_copy(held.at[i, c], targets[i].at[c], out_sem.at[i, j]) for i, j, c in cuts
    ]
    for load in loads:
        load.start()
    for load, store in zip(loads, stores):
        load.wait()
        store.start()
    for store in stores:
        store.wait()


def local(queries, keys, values, out_grad, tile_mask):
    groups = tile_mask.shape[0]
    nz = lax.axis_size("head")
    slab = queries.shape[0] * nz
    units = groups * 4
    out = jax.ShapeDtypeStruct((slab, groups * HD), BF16)
    hbm = pl.BlockSpec(memory_space=pl.ANY)
    dma = pltpu.SemaphoreType.DMA
    results = pl.pallas_call(
        functools.partial(kernel, groups),
        out_shape=(out,) * 4,
        in_specs=[hbm] * 5,
        out_specs=(hbm,) * 4,
        scratch_shapes=[
            pltpu.SMEM(tile_mask.shape, jnp.int32),
            pltpu.VMEM((4, 4, slab, groups * HD), BF16),
            pltpu.VMEM((units, slab, 4 * slab), BF16),
            pltpu.VMEM((groups * 8, 8, 8 * TILE), F32),
            pltpu.VMEM((4, slab, HD), F32),
            pltpu.VMEM((4, 16, 4 * slab), F32),
            pltpu.VMEM((4, 8, 4 * slab), F32),
            pltpu.VMEM((4, slab, HD), F32),
            pltpu.VMEM((4, slab, HD), F32),
            pltpu.VMEM((groups, 4 * slab, HD), BF16),
            pltpu.VMEM((4, 4, groups, slab, HD), BF16),
            pltpu.VMEM((4, groups, slab, HD), BF16),
            pltpu.VMEM((4, 2, groups, slab, HD), BF16),
            pltpu.VMEM((4, slab, groups * HD), BF16),
            dma((4,)),
            dma(()), dma((4, nz)), dma((4, nz)), dma((4,)), dma((4, 3)), dma((4, 3)),
            dma((3,)), dma((3,)), dma((3,)), dma((3,)),
            dma((4, 2)), dma((4, groups, 2)), dma((4, 2)), dma((4, 2)),
        ],
        compiler_params=pltpu.CompilerParams(
            collective_id=0, has_side_effects=True, vmem_limit_bytes=60 << 20
        ),
    )(queries, keys, values, out_grad, tile_mask)
    return pl.pallas_call(
        hand_over,
        out_shape=(out,) * 4,
        in_specs=[hbm] * 4,
        out_specs=(hbm,) * 4,
        scratch_shapes=[pltpu.VMEM((4, slab, groups * HD), BF16), dma((4, 2)), dma((4, 2))],
    )(*results)


def solution(mesh):
    return jax.shard_map(
        local,
        mesh=mesh,
        in_specs=(
            P(("dp", "frame", "head"), None),
            P(("dp", "frame", "head"), None),
            P(("dp", "frame", "head"), None),
            P(("dp", "frame", "head"), None),
            P("head", None, None),
        ),
        out_specs=(
            P(("dp", "frame"), "head"),
            P(("dp", "frame"), "head"),
            P(("dp", "frame"), "head"),
            P(("dp", "frame"), "head"),
        ),
        check_vma=False,
    )
```
